512 devices in a mesh: dp: 64 (over x, z_lo, core), seq: 8 (over y, z_hi).
Axes of the slice: x: 4, y: 4, z: 16 (z_hi: 2, z_lo: 8; z = z_hi * 8 + z_lo), core: 2. Of those that a mesh axis runs over, the one named last changes fastest.
Arguments:
- queries: bfloat16 [65536, 6144], P(('dp', 'seq')), may hold values from -8 to 8
- latent: bfloat16 [65536, 512], P(('dp', 'seq')), may hold values from -24 to 24
- key_rope: bfloat16 [65536, 64], P(('dp', 'seq')), may hold values from -8 to 8
- up_weight: bfloat16 [512, 8192], P(None, 'seq'), may hold values from -0.25 to 0.25
- out_grad: bfloat16 [65536, 4096], P(('dp', 'seq')), may hold values from -6 to 6
Outputs:
- latent_grad: float32 [65536, 512], P(('dp', 'seq'))
- weight_grad: float32 [512, 8192], P('dp', 'seq')
The draws below stay inside these ranges and needn't reach their ends.
All inputs are finite; a program needn't handle non-finite values.
Results may differ from the reference program's by a relative error of at most 0.0065.
Values may be sent and summed in bfloat16 or wider, within the bound.
No kernel may reach another device: no remote copies, remote signals or barrier semaphores. Data moves between devices by JAX's collectives and lax.ppermute only.
A program may use at most 64 MiB of HBM per device.

```python
import jax
import jax.numpy as jnp
from jax import lax

KV_RANK = 512
H = 32
NOPE = 128
ROPE = 64
VDIM = 128
LENGTH = 1024
TOKENS = 65536
N_DP = 64


def joint_draw(key):
    base_key = jax.random.fold_in(key, 7)
    query_key, rope_key = jax.random.split(base_key, 2)
    query_width = NOPE + ROPE
    queries = jnp.clip(jax.random.normal(query_key, (TOKENS, H * query_width), jnp.float32), -4.0, 4.0)
    rope = jnp.clip(jax.random.normal(rope_key, (TOKENS, ROPE), jnp.float32), -4.0, 4.0)
    return (queries, rope)


def draw_queries(key, part):
    return joint_draw(key)[0].astype(jnp.bfloat16)


def draw_key_rope(key, part):
    return joint_draw(key)[1].astype(jnp.bfloat16)


def raised(drawn, stream_key, source, target, blocks, factor):
    owner, partner = [(jnp.arange(drawn.shape[dim]) // (drawn.shape[dim] // blocks)).reshape([-1 if axis == dim else 1 for axis in range(drawn.ndim)]) for dim in (source, target)]
    chosen = jax.random.permutation(stream_key, blocks)[partner]
    strong = (owner == chosen) | (owner == (partner + blocks // 2) % blocks)
    return jnp.where(strong, factor * drawn, drawn)


def shard_levels(own_key, shape, shards, low, top_value):
    factor_of, own = 1.0, jax.random.fold_in(own_key, 6)
    for dim, blocks in shards:
        draws = jnp.exp(jax.random.uniform(jax.random.fold_in(own, dim), (blocks,), jnp.float32, low / len(shards), top_value / len(shards)))
        factor_of = factor_of * jnp.repeat(draws, shape[dim] // blocks).reshape([-1 if axis == dim else 1 for axis in range(len(shape))])
    return factor_of


def gaussian(stream_key, extent, width, most, cuts=(), dtype=jnp.bfloat16):
    level = shard_levels(stream_key, extent, cuts, -0.22, 0.18) if cuts else 1.0
    drawn = jax.random.normal(stream_key, extent, jnp.float32) * width * level
    return jnp.minimum(jnp.maximum(drawn, -most), most).astype(dtype)


def gaussian_with(key, extent, deviation, reach, shards, heavy, kind=jnp.bfloat16):
    entries = deviation * jax.random.normal(key, extent, jnp.float32)
    if shards:
        entries = entries * shard_levels(key, extent, shards, -0.22, 0.18)
    return jnp.clip(raised(entries, jax.random.fold_in(key, 3), *heavy), -reach, reach).astype(kind)


def setup_inputs(seed: int = 0) -> dict:
    streams_of = jax.random.split(jax.random.key(seed), 6)
    return {
        "queries": draw_queries(jax.random.fold_in(streams_of[5], 71), 0),
        "latent": gaussian_with(streams_of[1], (TOKENS, KV_RANK), 1.0, 24.0, ((0, 512),), (0, 1, 512, 6.0)),
        "key_rope": draw_key_rope(jax.random.fold_in(streams_of[5], 71), 0),
        "up_weight": gaussian(streams_of[3], (KV_RANK, H * (NOPE + VDIM)), KV_RANK ** -0.5, 0.25, ((1, 8),)),
        "out_grad": gaussian(streams_of[4], (TOKENS, H * VDIM), 1.0, 6.0, ((0, 512),)),
    }


def head_grads(query_head, kv_head, grad_head, rope_seq):
    score_scale = (NOPE + ROPE) ** -0.5
    query_nope = query_head[:, :NOPE]
    query_rope = query_head[:, NOPE:]
    keys_nope = kv_head[:, :NOPE]
    values = kv_head[:, NOPE:]
    scores = jnp.dot(query_nope, keys_nope.T, preferred_element_type=jnp.float32)
    scores = scores + jnp.dot(query_rope, rope_seq.T, preferred_element_type=jnp.float32)
    scores = scores * score_scale
    query_pos = lax.broadcasted_iota(jnp.int32, (LENGTH, LENGTH), 0)
    key_pos = lax.broadcasted_iota(jnp.int32, (LENGTH, LENGTH), 1)
    scores = jnp.where(key_pos <= query_pos, scores, jnp.float32(-1e30))
    row_max = jnp.max(scores, axis=1, keepdims=True)
    expo = jnp.exp(scores - row_max)
    probs = expo / jnp.sum(expo, axis=1, keepdims=True)
    probs_rounded = probs.astype(jnp.bfloat16)
    value_grad = jnp.dot(probs_rounded.T, grad_head, preferred_element_type=jnp.float32)
    prob_grad = jnp.dot(grad_head, values.T, preferred_element_type=jnp.float32)
    row_dot = jnp.sum(probs * prob_grad, axis=1, keepdims=True)
    score_grad = (probs * (prob_grad - row_dot) * score_scale).astype(jnp.bfloat16)
    key_grad = jnp.dot(score_grad.T, query_nope, preferred_element_type=jnp.float32)
    return jnp.concatenate([key_grad, value_grad], axis=1).astype(jnp.bfloat16)


def reference(queries, latent, key_rope, up_weight, out_grad):
    query_width = NOPE + ROPE
    kv_width = NOPE + VDIM

    def one_sequence(total, inputs):
        latent_seq, rope_seq, query_seq, grad_seq = inputs
        kv_cols = jnp.dot(latent_seq, up_weight, preferred_element_type=jnp.float32).astype(jnp.bfloat16)
        stacked = (query_seq.reshape(LENGTH, H, query_width).transpose(1, 0, 2),
                   kv_cols.reshape(LENGTH, H, kv_width).transpose(1, 0, 2),
                   grad_seq.reshape(LENGTH, H, VDIM).transpose(1, 0, 2))
        head_cols = lax.map(lambda parts: head_grads(parts[0], parts[1], parts[2], rope_seq), stacked)
        grad_cols = head_cols.transpose(1, 0, 2).reshape(LENGTH, H * kv_width)
        latent_seq_grad = jnp.dot(grad_cols, up_weight.T, preferred_element_type=jnp.float32)
        total = total + jnp.dot(latent_seq.T, grad_cols, preferred_element_type=jnp.float32)
        return total, latent_seq_grad

    inputs = (latent.reshape(N_DP, LENGTH, KV_RANK), key_rope.reshape(N_DP, LENGTH, ROPE),
              queries.reshape(N_DP, LENGTH, H * query_width), out_grad.reshape(N_DP, LENGTH, H * VDIM))
    start_total = jnp.zeros((KV_RANK, H * kv_width), jnp.float32)
    total, latent_parts = lax.scan(one_sequence, start_total, inputs)
    return latent_parts.reshape(TOKENS, KV_RANK), total / N_DP
```

```python
import functools
import math

import jax
import jax.numpy as jnp
from jax import lax
from jax.experimental import pallas as pl
from jax.experimental.pallas import tpu as pltpu
from jax.sharding import Mesh
from jax.sharding import PartitionSpec as P

NOPE = 128
ROPE = 64
VDIM = 128
QW = NOPE + ROPE
KVW = NOPE + VDIM
RANK = 512
SCALE = QW ** (-0.5)
BF16 = jnp.bfloat16
F32 = jnp.float32
NT = (((1,), (1,)), ((), ()))


def head_pair(kv, rope, q2, g2, w, bias, lat_t):
    length = kv.shape[0]
    half = length // 2
    weight_parts = []
    latent_sum = None
    for h in range(2):
        keys = kv[:, h * KVW : h * KVW + NOPE]
        values = kv[:, h * KVW + NOPE : (h + 1) * KVW]
        keys_full = jnp.concatenate([keys, rope], axis=1)
        query = q2[:, h * QW : (h + 1) * QW]
        query_nope = query[:, :NOPE]
        grad = g2[:, h * VDIM : (h + 1) * VDIM]
        key_grad = [None, None]
        value_grad = [None, None]
        rows_each = half // 2
        for part in range(2):
            rows = slice(part * rows_each, (part + 1) * rows_each)
            n_keys = half * (part + 1)
            scores = lax.dot_general(
                keys_full[:n_keys], query[rows], NT, preferred_element_type=F32
            )
            masked = scores[n_keys - half :] + bias
            scores = masked if part == 0 else jnp.concatenate([scores[:half], masked], axis=0)
            row_max = jnp.max(scores, axis=0, keepdims=True)
            expo = jnp.exp2((scores - row_max) * (SCALE * math.log2(math.e)))
            probs = expo * (1.0 / jnp.sum(expo, axis=0, keepdims=True))
            probs_rounded = probs.astype(BF16)
            prob_grad = lax.dot_general(
                values[:n_keys], grad[rows], NT, preferred_element_type=F32
            )
            row_dot = jnp.sum(probs * prob_grad, axis=0, keepdims=True)
            score_grad = (probs * (prob_grad - row_dot)).astype(BF16)
            for block in range(part + 1):
                cut = slice(block * half, (block + 1) * half)
                value_part = jnp.dot(probs_rounded[cut], grad[rows], preferred_element_type=F32)
                key_part = jnp.dot(score_grad[cut], query_nope[rows], preferred_element_type=F32)
                if value_grad[block] is None:
                    value_grad[block], key_grad[block] = value_part, key_part
                else:
                    value_grad[block] = value_grad[block] + value_part
                    key_grad[block] = key_grad[block] + key_part
        grad_cols = jnp.concatenate(
            [
                jnp.concatenate([key_grad[b] * SCALE, value_grad[b]], axis=1).astype(BF16)
                for b in range(2)
            ],
            axis=0,
        )
        weight_parts.append(jnp.dot(lat_t, grad_cols, preferred_element_type=F32).astype(BF16))
        latent_part = lax.dot_general(
            grad_cols, w[:, h * KVW : (h + 1) * KVW], NT, preferred_element_type=F32
        )
        latent_sum = latent_part if latent_sum is None else latent_sum + latent_part
    return weight_parts, latent_sum


def attention_kernel(first, last, n_core, n_x, n_zl, rows_each, *refs):
    place_ref, lat_ref, w_ref = refs[:3]
    q_refs, g_refs = refs[3:7], refs[7:11]
    refs = refs[11:]
    if not first:
        acc_ref, before, refs = refs[0], refs[1:3], refs[3:]
    grad_refs = refs[:2]
    lg_refs = refs[2:-5]
    bias, lat_t, total, queries, grads = refs[-5:]
    step = pl.program_id(0)
    zh, y, core = place_ref[0], place_ref[1], place_ref[2]

    @pl.when(step == 0)
    def _():
        key_pos = lax.broadcasted_iota(jnp.int32, bias.shape, 0)
        lane = lax.broadcasted_iota(jnp.int32, bias.shape, 1)
        block = jnp.where(lane >= 128, 2, 0) + zh
        query_pos = block * 128 + (lane & 127)
        bias[...] = jnp.where(key_pos <= query_pos, F32(0.0), F32(-1e30))
        row = lax.broadcasted_iota(jnp.int32, (RANK, RANK), 0)
        col = lax.broadcasted_iota(jnp.int32, (RANK, RANK), 1)
        inner = row % rows_each
        zl = (row // rows_each) % n_zl
        x = (row // (rows_each * n_zl)) % n_x
        away = row // (rows_each * n_zl * n_x)
        owner = core + away * (1 - 2 * core)
        source = ((x * n_zl + zl) * n_core + owner) * rows_each + inner
        pick = jnp.where(source == col, F32(1.0), F32(0.0)).astype(BF16)
        lat_t[...] = lax.dot_general(
            pick, lat_ref[:, :RANK], NT, preferred_element_type=F32
        ).astype(BF16)
        total[...] = jnp.zeros_like(total) if first else acc_ref[...]

    n_y = len(q_refs)
    tokens = q_refs[0].shape[0]
    for k in range(n_y):
        start = pl.multiple_of(((y + n_y - k) % n_y) * tokens, tokens)
        queries[pl.ds(start, tokens), :] = q_refs[k][...]
        grads[pl.ds(start, tokens), :] = g_refs[k][...]
    w = w_ref[...]
    kv = jnp.dot(lat_ref[:, :RANK], w, preferred_element_type=F32).astype(BF16)
    weight_parts, latent_sum = head_pair(
        kv, lat_ref[:, RANK : RANK + ROPE], queries[...], grads[...], w, bias[...], lat_t[...]
    )
    half = RANK // n_core
    for away, ref in enumerate(grad_refs):
        if not first:
            ref[:, pl.ds(zh, 1)] = before[away][...][:, None]
        for h in range(2):
            part = weight_parts[h][away * half : (away + 1) * half].reshape(n_x, -1, KVW)
            if first:
                ref[:, :, h * KVW : (h + 1) * KVW] = part
            else:
                ref[:, pl.ds(1 - zh, 1), :, h * KVW : (h + 1) * KVW] = part[:, None]
    total[...] += latent_sum

    @pl.when(step == pl.num_programs(0) - 1)
    def _():
        if not last:
            lg_refs[0][...] = total[...]
            return
        rows = total.shape[0] // n_y
        for k in range(n_y):
            start = pl.multiple_of(((y + k) % n_y) * rows, rows)
            lg_refs[k][...] = total[pl.ds(start, rows), :].astype(BF16)


def attention(place, lat, weight, queries, out_grad, arrived, before, sizes):
    length = lat.shape[0]
    heads = weight.shape[1] // KVW
    first = own = before is None
    last = not first
    n_core, n_x, n_zl = sizes
    n_y = len(arrived) + 1
    steps = heads // 2
    rows_each = RANK // (n_core * n_x * n_zl)
    tokens = queries.shape[0]
    q_blocks = heads * QW // (2 * VDIM)

    def column(i, place_ref):
        which = place_ref[0] if own else 1 - place_ref[0]
        return (place_ref[1] * 2 + which) * steps + i

    specs = [
        pl.BlockSpec((length, lat.shape[1]), lambda i, p: (0, 0)),
        pl.BlockSpec((RANK, 2 * KVW), lambda i, p: (0, i)),
        pl.BlockSpec((tokens, 2 * QW), lambda i, p: (0, column(i, p))),
        *[pl.BlockSpec((tokens, 2 * QW), lambda i, p: (0, i)) for _ in arrived],
        pl.BlockSpec((tokens, 2 * VDIM), lambda i, p: (0, column(i, p))),
        *[pl.BlockSpec((tokens, 2 * VDIM), lambda i, p: (0, q_blocks + i)) for _ in arrived],
    ]
    args = [lat, weight, queries, *arrived, out_grad, *arrived]
    rows = RANK // (n_core * n_x)
    grad_spec = pl.BlockSpec((n_x, rows, 2 * KVW), lambda i, p: (0, 0, i))
    grad_shape = jax.ShapeDtypeStruct((n_x, rows, heads * KVW), BF16)
    if not first:
        specs.append(pl.BlockSpec((length, RANK), lambda i, p: (0, 0)))
        specs.extend([grad_spec] * 2)
        args.extend(before)
        grad_spec = pl.BlockSpec((n_x, 2, rows, 2 * KVW), lambda i, p: (0, 0, 0, i))
        grad_shape = jax.ShapeDtypeStruct((n_x, 2, rows, heads * KVW), BF16)
    flops = heads * (3 * 2 * length * RANK * KVW + 4 * 2 * length * tokens * n_y * 192)
    if last:
        rows = length // n_y
        latent_specs = [pl.BlockSpec((rows, RANK), lambda i, p: (0, 0))] * n_y
        latent_shapes = [jax.ShapeDtypeStruct((rows, RANK), BF16)] * n_y
    else:
        latent_specs = [pl.BlockSpec((length, RANK), lambda i, p: (0, 0))]
        latent_shapes = [jax.ShapeDtypeStruct((length, RANK), F32)]
    keep, send, *latent_parts = pl.pallas_call(
        functools.partial(attention_kernel, first, last, n_core, n_x, n_zl, rows_each),
        grid_spec=pltpu.PrefetchScalarGridSpec(
            num_scalar_prefetch=1,
            grid=(steps,),
            in_specs=specs,
            out_specs=[grad_spec, grad_spec, *latent_specs],
            scratch_shapes=[
                pltpu.VMEM((length // 2, length // 4), F32),
                pltpu.VMEM((RANK, length), BF16),
                pltpu.VMEM((length, RANK), F32),
                pltpu.VMEM((tokens * n_y, 2 * QW), BF16),
                pltpu.VMEM((tokens * n_y, 2 * VDIM), BF16),
            ],
        ),
        out_shape=[grad_shape, grad_shape, *latent_shapes],
        compiler_params=pltpu.CompilerParams(
            dimension_semantics=("arbitrary",), vmem_limit_bytes=56 * 2**20
        ),
        cost_estimate=pl.CostEstimate(
            flops=flops, bytes_accessed=12 * 2**20, transcendentals=heads * length * tokens * n_y
        ),
    )(place, *args)
    return keep, send, latent_parts


def split_kernel(count, place_ref, *refs):
    outs = refs[2 * count :]
    for k in range(count):
        width = refs[k].shape[1]
        outs[k][:, :width] = refs[k][...]
        outs[k][:, width:] = refs[count + k][...]


def split_heads(place, queries, out_grad, own, n_y, n_zh):
    tokens = queries.shape[0]
    parts = n_y * n_zh
    count = n_y - 1
    widths = (queries.shape[1] // parts, out_grad.shape[1] // parts)

    def block(width, k):
        def index(i, place_ref):
            which = place_ref[0] if own else 1 - place_ref[0]
            return (0, ((place_ref[1] + k + 1) % n_y) * n_zh + which)

        return pl.BlockSpec((tokens, width), index)

    return pl.pallas_call(
        functools.partial(split_kernel, count),
        grid_spec=pltpu.PrefetchScalarGridSpec(
            num_scalar_prefetch=1,
            grid=(1,),
            in_specs=[block(width, k) for width in widths for k in range(count)],
            out_specs=[pl.BlockSpec((tokens, sum(widths)), lambda i, p: (0, 0))] * count,
        ),
        out_shape=[jax.ShapeDtypeStruct((tokens, sum(widths)), BF16)] * count,
        cost_estimate=pl.CostEstimate(
            flops=0, bytes_accessed=4 * count * tokens * sum(widths), transcendentals=0
        ),
    )(place, *[queries] * count, *[out_grad] * count)


def latent_kernel(latent_ref, rope_ref, out_ref):
    rope = rope_ref[...].astype(F32).T.astype(BF16)
    rest = out_ref.shape[2] - RANK - ROPE
    joined = jnp.concatenate([rope, jnp.zeros((rope.shape[0], rest), BF16)], axis=1)
    for k in range(out_ref.shape[0]):
        out_ref[k, :, :RANK] = latent_ref[...]
        out_ref[k, :, RANK:] = joined


def latent_copies(latent, rope, count):
    shape = (count, latent.shape[0], RANK + 2 * ROPE)
    return pl.pallas_call(
        latent_kernel,
        out_shape=jax.ShapeDtypeStruct(shape, BF16),
        cost_estimate=pl.CostEstimate(
            flops=0, bytes_accessed=2 * math.prod(shape), transcendentals=0
        ),
    )(latent, rope.T)


def rotate(array, axis, shift):
    n = lax.axis_size(axis)
    return lax.ppermute(array, axis, [(i, (i + shift) % n) for i in range(n)])


def exchange(pieces, axes):
    return lax.all_to_all(pieces, axes, split_axis=0, concat_axis=0, tiled=True)


def add_up(pieces, dtype=BF16):
    return jnp.sum(pieces.astype(F32), axis=0).astype(dtype)


def to_all(array, axes, count):
    return exchange(jnp.broadcast_to(array[None], (count,) + array.shape), axes)


def per_device(queries, latent, key_rope, up_weight, out_grad):
    n_x, n_zl, n_core = lax.axis_size("x"), lax.axis_size("zl"), lax.axis_size("core")
    n_y, n_zh = lax.axis_size("y"), lax.axis_size("zh")
    zh, y, core = lax.axis_index("zh"), lax.axis_index("y"), lax.axis_index("core")
    place = jnp.stack([zh, y, core]).astype(jnp.int32)
    tokens = latent.shape[0]

    copies = latent_copies(latent, key_rope, n_y * n_zh)
    lat = exchange(copies, ("y", "zh")).reshape(n_y * n_zh * tokens, copies.shape[2])

    piece_rows = RANK // (n_x * n_core)
    mine = lax.axis_index("x") * n_core + core
    piece = lax.dynamic_slice_in_dim(up_weight, mine * piece_rows, piece_rows, 0)
    other_weight = to_all(rotate(piece, "zh", 1), ("x", "core"), n_x * n_core)
    other_weight = other_weight.reshape(up_weight.shape)

    own = split_heads(place, queries, out_grad, True, n_y, n_zh)
    other = split_heads(place, queries, out_grad, False, n_y, n_zh)
    own = [rotate(a, "y", k + 1) for k, a in enumerate(own)]
    other = [rotate(a, "y", k + 1) for k, a in enumerate(other)]
    sizes = (n_core, n_x, n_zl)
    keep, send, parts = attention(place, lat, up_weight, queries, out_grad, own, None, sizes)
    keep, send, parts = attention(
        place, lat, other_weight, queries, out_grad, other, [parts[0], keep, send], sizes
    )
    on_chip = (keep.astype(F32) + rotate(send, "core", 1).astype(F32)).astype(BF16)
    arrived = [parts[0]] + [rotate(a, "y", k + 1) for k, a in enumerate(parts[1:])]

    latent_sum = sum(a.astype(F32) for a in arrived).reshape(n_zh, tokens, RANK)
    sent = lax.dynamic_index_in_dim(latent_sum, 1 - zh, 0, keepdims=False).astype(BF16)
    kept = lax.dynamic_index_in_dim(latent_sum, zh, 0, keepdims=False)
    latent_grad = kept + rotate(sent, "zh", 1).astype(F32)

    over_x, _ = lax.optimization_barrier((add_up(exchange(on_chip, "x")), sent))
    pieces = over_x.reshape(n_zh * n_zl, -1, over_x.shape[2])
    weight_grad = add_up(exchange(pieces, ("zh", "zl")), F32)
    return latent_grad, weight_grad * (1.0 / (n_x * n_zl * n_core))


def solution(mesh):
    replicas, parts = mesh.shape["dp"], mesh.shape["seq"]
    shape = (replicas // 16, 8, 2, parts // 2, 2)
    names = ("x", "zl", "core", "y", "zh")
    torus = Mesh(mesh.devices.reshape(shape), names)
    rows = P(names, None)
    in_specs = (rows, rows, rows, P(None, ("y", "zh")), rows)
    out_specs = (rows, P(("x", "zl", "core"), ("y", "zh")))
    return jax.shard_map(
        per_device, mesh=torus, in_specs=in_specs, out_specs=out_specs, check_vma=False
    )
```

```python
import functools
import math

import jax
import jax.numpy as jnp
from jax import lax
from jax.experimental import pallas as pl
from jax.experimental.pallas import tpu as pltpu
from jax.sharding import Mesh
from jax.sharding import PartitionSpec as P

NOPE = 128
ROPE = 64
VDIM = 128
QW = NOPE + ROPE
KVW = NOPE + VDIM
RANK = 512
SCALE = QW ** (-0.5)
BF16 = jnp.bfloat16
F32 = jnp.float32
NT = (((1,), (1,)), ((), ()))


def head_pair(kv, rope, q2, g2, w, bias, lat_t):
    length = kv.shape[0]
    half = length // 2
    weight_parts = []
    latent_sum = None
    for h in range(2):
        keys = kv[:, h * KVW : h * KVW + NOPE]
        values = kv[:, h * KVW + NOPE : (h + 1) * KVW]
        keys_full = jnp.concatenate([keys, rope], axis=1)
        query = q2[:, h * QW : (h + 1) * QW]
        query_nope = query[:, :NOPE]
        grad = g2[:, h * VDIM : (h + 1) * VDIM]
        key_grad = [None, None]
        value_grad = [None, None]
        rows_each = half // 2
        for part in range(2):
            rows = slice(part * rows_each, (part + 1) * rows_each)
            n_keys = half * (part + 1)
            scores = lax.dot_general(
                keys_full[:n_keys], query[rows], NT, preferred_element_type=F32
            )
            masked = scores[n_keys - half :] + bias
            scores = masked if part == 0 else jnp.concatenate([scores[:half], masked], axis=0)
            row_max = jnp.max(scores, axis=0, keepdims=True)
            expo = jnp.exp2((scores - row_max) * (SCALE * math.log2(math.e)))
            probs = expo * (1.0 / jnp.sum(expo, axis=0, keepdims=True))
            probs_rounded = probs.astype(BF16)
            prob_grad = lax.dot_general(
                values[:n_keys], grad[rows], NT, preferred_element_type=F32
            )
            row_dot = jnp.sum(probs * prob_grad, axis=0, keepdims=True)
            score_grad = (probs * (prob_grad - row_dot)).astype(BF16)
            for block in range(part + 1):
                cut = slice(block * half, (block + 1) * half)
                value_part = jnp.dot(probs_rounded[cut], grad[rows], preferred_element_type=F32)
                key_part = jnp.dot(score_grad[cut], query_nope[rows], preferred_element_type=F32)
                if value_grad[block] is None:
                    value_grad[block], key_grad[block] = value_part, key_part
                else:
                    value_grad[block] = value_grad[block] + value_part
                    key_grad[block] = key_grad[block] + key_part
        grad_cols = jnp.concatenate(
            [
                jnp.concatenate([key_grad[b] * SCALE, value_grad[b]], axis=1).astype(BF16)
                for b in range(2)
            ],
            axis=0,
        )
        weight_parts.append(jnp.dot(lat_t, grad_cols, preferred_element_type=F32).astype(BF16))
        latent_part = lax.dot_general(
            grad_cols, w[:, h * KVW : (h + 1) * KVW], NT, preferred_element_type=F32
        )
        latent_sum = latent_part if latent_sum is None else latent_sum + latent_part
    return weight_parts, latent_sum


def attention_kernel(n_core, n_x, n_zl, n_y, place_ref, *refs):
    mine_ref, lat_refs, refs = refs[0], refs[1 : n_y + 1], refs[n_y + 1 :]
    q_ref, g_ref, own_w_ref, other_w_ref, keep_ref, send_ref = refs[:6]
    lg_refs = refs[6 : n_y + 6]
    lat, bias, lat_t, total, weight = refs[n_y + 6 :]
    step = pl.program_id(0)
    zh, y, core = place_ref[0], place_ref[1], place_ref[2]
    rows = total.shape[0] // n_y
    tokens = rows // 2

    @pl.when(step == 0)
    def _():
        for k in range(n_y):
            start = pl.multiple_of((k * 2 + zh) * tokens, tokens)
            lat[pl.ds(start, tokens), :] = mine_ref[k * tokens : (k + 1) * tokens]
            start = pl.multiple_of((((y + n_y - k) % n_y) * 2 + 1 - zh) * tokens, tokens)
            lat[pl.ds(start, tokens), :] = lat_refs[k][...]
        key_pos = lax.broadcasted_iota(jnp.int32, bias.shape, 0)
        lane = lax.broadcasted_iota(jnp.int32, bias.shape, 1)
        block = jnp.where(lane >= 128, 2, 0) + zh
        query_pos = block * 128 + (lane & 127)
        bias[...] = jnp.where(key_pos <= query_pos, F32(0.0), F32(-1e30))
        rows_each = RANK // (n_core * n_x * n_zl)
        row = lax.broadcasted_iota(jnp.int32, (RANK, RANK), 0)
        col = lax.broadcasted_iota(jnp.int32, (RANK, RANK), 1)
        inner = row % rows_each
        zl = (row // rows_each) % n_zl
        x = (row // (rows_each * n_zl)) % n_x
        away = row // (rows_each * n_zl * n_x)
        owner = core + away * (1 - 2 * core)
        wanted = ((x * n_zl + zl) * n_core + owner) * rows_each + inner
        pick = jnp.where(wanted == col, F32(1.0), F32(0.0)).astype(BF16)
        lat_t[...] = lax.dot_general(pick, lat[:, :RANK], NT, preferred_element_type=F32).astype(
            BF16
        )
        total[...] = jnp.zeros_like(total)

    held = step // (pl.num_programs(0) // 2) == zh

    @pl.when(held)
    def _():
        weight[...] = own_w_ref[...]

    @pl.when(jnp.logical_not(held))
    def _():
        weight[...] = other_w_ref[...]

    w = weight[...]
    kv = jnp.dot(lat[:, :RANK], w, preferred_element_type=F32).astype(BF16)
    weight_parts, latent_sum = head_pair(
        kv, lat[:, RANK : RANK + ROPE], q_ref[...], g_ref[...], w, bias[...], lat_t[...]
    )
    half = RANK // n_core
    for away, ref in enumerate((keep_ref, send_ref)):
        for h in range(2):
            part = weight_parts[h][away * half : (away + 1) * half].reshape(n_x, -1, KVW)
            ref[:, 0, :, h * KVW : (h + 1) * KVW] = part
    total[...] += latent_sum

    @pl.when(step == pl.num_programs(0) - 1)
    def _():
        for k in range(n_y):
            start = pl.multiple_of(((y + k) % n_y) * rows, rows)
            lg_refs[k][...] = total[pl.ds(start, rows), :].astype(BF16)


def attention(place, latents, query_grad, own_weight, other_weight, sizes):
    n_core, n_x, n_zl = sizes
    n_y = len(latents)
    q_rows, width = query_grad.shape[0], latents[0].shape[1]
    length = 2 * q_rows
    heads = 2 * own_weight.shape[1] // KVW
    steps = heads // 2
    g_blocks = heads * QW // (2 * VDIM)
    rows = RANK // (n_core * n_x)
    lat_spec = pl.BlockSpec((q_rows // n_y, width), lambda i, p: (0, 0))
    lat_block = heads * (QW + VDIM) // width
    w_spec = pl.BlockSpec((RANK, 2 * KVW), lambda i, p: (0, i % (steps // 2)))
    grad_spec = pl.BlockSpec(
        (n_x, 1, rows, 2 * KVW), lambda i, p: (0, i // (steps // 2), 0, i % (steps // 2))
    )
    grad_shape = jax.ShapeDtypeStruct((n_x, 2, rows, heads * KVW // 2), BF16)
    part_spec = pl.BlockSpec((length // n_y, RANK), lambda i, p: (0, 0))
    part_shape = jax.ShapeDtypeStruct((length // n_y, RANK), BF16)
    flops = heads * (3 * 2 * length * RANK * KVW + 4 * 2 * length * q_rows * 192)
    keep, send, *parts = pl.pallas_call(
        functools.partial(attention_kernel, n_core, n_x, n_zl, n_y),
        grid_spec=pltpu.PrefetchScalarGridSpec(
            num_scalar_prefetch=1,
            grid=(steps,),
            in_specs=[
                pl.BlockSpec((q_rows, width), lambda i, p: (0, lat_block)),
                *[lat_spec] * n_y,
                pl.BlockSpec((q_rows, 2 * QW), lambda i, p: (0, i)),
                pl.BlockSpec((q_rows, 2 * VDIM), lambda i, p: (0, g_blocks + i)),
                w_spec,
                w_spec,
            ],
            out_specs=[grad_spec, grad_spec, *[part_spec] * n_y],
            scratch_shapes=[
                pltpu.VMEM((length, width), BF16),
                pltpu.VMEM((length // 2, length // 4), F32),
                pltpu.VMEM((RANK, length), BF16),
                pltpu.VMEM((length, RANK), F32),
                pltpu.VMEM((RANK, 2 * KVW), BF16),
            ],
        ),
        out_shape=[grad_shape, grad_shape, *[part_shape] * n_y],
        compiler_params=pltpu.CompilerParams(
            dimension_semantics=("arbitrary",), vmem_limit_bytes=56 * 2**20
        ),
        cost_estimate=pl.CostEstimate(
            flops=flops, bytes_accessed=16 * 2**20, transcendentals=heads * length * q_rows
        ),
    )(place, query_grad, *latents, query_grad, query_grad, own_weight, other_weight)
    return keep, send, parts


def split_kernel(queries_ref, grads_ref, latent_ref, out_ref):
    offset = 0
    for ref in (queries_ref, grads_ref, latent_ref):
        out_ref[0, :, offset : offset + ref.shape[1]] = ref[...]
        offset += ref.shape[1]


def split_heads(queries, out_grad, packed, n_y):
    tokens = queries.shape[0]
    widths = (queries.shape[1] // n_y, out_grad.shape[1] // n_y, RANK + 2 * ROPE)
    shape = (n_y, tokens, sum(widths))
    return pl.pallas_call(
        split_kernel,
        grid=(n_y,),
        in_specs=[
            pl.BlockSpec((tokens, widths[0]), lambda i: (0, i)),
            pl.BlockSpec((tokens, widths[1]), lambda i: (0, i)),
            pl.BlockSpec((tokens, widths[2]), lambda i: (0, 0)),
        ],
        out_specs=pl.BlockSpec((1,) + shape[1:], lambda i: (i, 0, 0)),
        out_shape=jax.ShapeDtypeStruct(shape, BF16),
        cost_estimate=pl.CostEstimate(
            flops=0, bytes_accessed=4 * math.prod(shape), transcendentals=0
        ),
    )(queries, out_grad, packed)


def pack_kernel(place_ref, latent_ref, rope_ref, weight_ref, out_ref):
    tokens, rank = latent_ref.shape
    rope = rope_ref[...].astype(F32).T.astype(BF16)
    out_ref[:, :rank] = latent_ref[...]
    out_ref[:, rank : rank + 2 * ROPE] = jnp.concatenate([rope, jnp.zeros_like(rope)], axis=1)
    rows, width = weight_ref.shape
    for half in range(tokens // rows):
        columns = weight_ref[:, half * width // 2 : (half + 1) * width // 2]
        out_ref[half * rows : (half + 1) * rows, rank + 2 * ROPE :] = columns


def pack(place, latent, rope, weight, pieces):
    tokens, rank = latent.shape
    rows, width = weight.shape[0] // pieces, weight.shape[1]
    shape = (tokens, rank + 2 * ROPE + width // 2)
    return pl.pallas_call(
        pack_kernel,
        grid_spec=pltpu.PrefetchScalarGridSpec(
            num_scalar_prefetch=1,
            grid=(1,),
            in_specs=[
                pl.BlockSpec((tokens, rank), lambda i, p: (0, 0)),
                pl.BlockSpec((ROPE, tokens), lambda i, p: (0, 0)),
                pl.BlockSpec((rows, width), lambda i, p: (p[3], 0)),
            ],
            out_specs=pl.BlockSpec(shape, lambda i, p: (0, 0)),
        ),
        out_shape=jax.ShapeDtypeStruct(shape, BF16),
        cost_estimate=pl.CostEstimate(
            flops=0, bytes_accessed=4 * math.prod(shape), transcendentals=0
        ),
    )(place, latent, rope.T, weight)


def unpack_kernel(other_ref, lat_ref, weight_ref):
    width = lat_ref.shape[1]
    lat_ref[...] = other_ref[:, :width]
    count, rows, columns = weight_ref.shape
    for k in range(count):
        for half in range(2):
            part = other_ref[half * rows : (half + 1) * rows, width:]
            weight_ref[k, :, half * columns // 2 : (half + 1) * columns // 2] = part


def unpack(other, count, piece_rows):
    tokens, width = other.shape
    latent_width = RANK + 2 * ROPE
    piece = (count, piece_rows, (width - latent_width) * tokens // piece_rows)
    return pl.pallas_call(
        unpack_kernel,
        out_shape=[
            jax.ShapeDtypeStruct((tokens, latent_width), BF16),
            jax.ShapeDtypeStruct(piece, BF16),
        ],
        cost_estimate=pl.CostEstimate(
            flops=0, bytes_accessed=3 * math.prod(piece), transcendentals=0
        ),
    )(other)


def rotate(array, axis, shift):
    n = lax.axis_size(axis)
    return lax.ppermute(array, axis, [(i, (i + shift) % n) for i in range(n)])


def exchange(pieces, axes):
    return lax.all_to_all(pieces, axes, split_axis=0, concat_axis=0, tiled=True)


def add_up(pieces, dtype=BF16):
    return jnp.sum(pieces.astype(F32), axis=0).astype(dtype)


def per_device(queries, latent, key_rope, up_weight, out_grad):
    n_x, n_zl, n_core = lax.axis_size("x"), lax.axis_size("zl"), lax.axis_size("core")
    n_y, n_zh = lax.axis_size("y"), lax.axis_size("zh")
    zh, y, core = lax.axis_index("zh"), lax.axis_index("y"), lax.axis_index("core")
    mine = lax.axis_index("x") * n_core + core
    place = jnp.stack([zh, y, core, mine]).astype(jnp.int32)
    tokens = latent.shape[0]
    pieces = n_x * n_core

    packed = pack(place, latent, key_rope, up_weight, pieces)
    sent = split_heads(queries, out_grad, packed, n_y)
    query_grad = exchange(sent, "y").reshape(n_y * tokens, -1)
    latents, piece = unpack(rotate(packed, "zh", 1), pieces, RANK // pieces)
    latents = [latents] + [rotate(latents, "y", k + 1) for k in range(n_y - 1)]
    piece, query_grad = lax.optimization_barrier((piece, query_grad))
    other_weight = exchange(piece, ("x", "core")).reshape(up_weight.shape)

    sizes = (n_core, n_x, n_zl)
    keep, send, parts = attention(place, latents, query_grad, up_weight, other_weight, sizes)
    on_chip = (keep.astype(F32) + rotate(send, "core", 1).astype(F32)).astype(BF16)
    arrived = [parts[0]] + [rotate(a, "y", k + 1) for k, a in enumerate(parts[1:])]

    latent_sum = sum(a.astype(F32) for a in arrived).reshape(n_zh, tokens, RANK)
    sent = lax.dynamic_index_in_dim(latent_sum, 1 - zh, 0, keepdims=False).astype(BF16)
    kept = lax.dynamic_index_in_dim(latent_sum, zh, 0, keepdims=False)
    sent = rotate(sent, "zh", 1)
    latent_grad = kept + sent.astype(F32)

    over_x, _ = lax.optimization_barrier((add_up(exchange(on_chip, "x")), sent))
    over_x = over_x.reshape(n_zh, n_zl, -1, over_x.shape[2]).swapaxes(0, 1)
    over_x = over_x.reshape(n_zh * n_zl, -1, over_x.shape[3])
    weight_grad = add_up(exchange(over_x, ("zl", "zh")), F32)
    return latent_grad, weight_grad * (1.0 / (n_x * n_zl * n_core))


def solution(mesh):
    replicas, parts = mesh.shape["dp"], mesh.shape["seq"]
    shape = (replicas // 16, 8, 2, parts // 2, 2)
    names = ("x", "zl", "core", "y", "zh")
    torus = Mesh(mesh.devices.reshape(shape), names)
    rows = P(names, None)
    in_specs = (rows, rows, rows, P(None, ("y", "zh")), rows)
    out_specs = (rows, P(("x", "zl", "core"), ("y", "zh")))
    return jax.shard_map(
        per_device, mesh=torus, in_specs=in_specs, out_specs=out_specs, check_vma=False
    )
```

```python
import functools
import math

import jax
import jax.numpy as jnp
from jax import lax
from jax.experimental import pallas as pl
from jax.experimental.pallas import tpu as pltpu
from jax.sharding import Mesh
from jax.sharding import PartitionSpec as P

NOPE = 128
ROPE = 64
VDIM = 128
QW = NOPE + ROPE
KVW = NOPE + VDIM
RANK = 512
SCALE = QW ** (-0.5)
BF16 = jnp.bfloat16
F32 = jnp.float32
NT = (((1,), (1,)), ((), ()))


def head_pair(kv, rope, q2, g2, w, bias, lat_t):
    half = kv.shape[0] // 2
    rows_each = half // 2
    grad_cols = [[[None, None], [None, None]] for _ in range(2)]

    def products(h, part):
        n_keys = half * (part + 1)
        rows = slice(part * rows_each, (part + 1) * rows_each)
        keys = jnp.concatenate([kv[:n_keys, h * KVW : h * KVW + NOPE], rope[:n_keys]], axis=1)
        values = kv[:n_keys, h * KVW + NOPE : (h + 1) * KVW]
        query = q2[rows, h * QW : (h + 1) * QW]
        grad = g2[rows, h * VDIM : (h + 1) * VDIM]
        scores = lax.dot_general(keys, query, NT, preferred_element_type=F32)
        prob_grad = lax.dot_general(values, grad, NT, preferred_element_type=F32)
        return scores, prob_grad, query[:, :NOPE], grad

    def softmax(part, scores, prob_grad):
        if part == 0:
            scores = scores + bias
        else:
            scores = jnp.concatenate([scores[:half], scores[half:] + bias], axis=0)
        row_max = jnp.max(scores, axis=0, keepdims=True)
        expo = jnp.exp2((scores - row_max) * (SCALE * math.log2(math.e)))
        probs = expo * (1.0 / jnp.sum(expo, axis=0, keepdims=True))
        row_dot = jnp.sum(probs * prob_grad, axis=0, keepdims=True)
        return probs.astype(BF16), (probs * (prob_grad - row_dot)).astype(BF16)

    def accumulate(h, part, probs, score_grad, query_nope, grad):
        for block in range(part + 1):
            cut = slice(block * half, (block + 1) * half)
            for which, (left, right) in enumerate(((score_grad, query_nope), (probs, grad))):
                product = jnp.dot(left[cut], right, preferred_element_type=F32)
                before = grad_cols[h][block][which]
                grad_cols[h][block][which] = product if before is None else before + product

    units = [(h, part) for h in range(2) for part in (1, 0)]
    ready = products(*units[0])
    for n, (h, part) in enumerate(units):
        scores, prob_grad, query_nope, grad = ready
        if n + 1 < len(units):
            ready = products(*units[n + 1])
        probs, score_grad = softmax(part, scores, prob_grad)
        accumulate(h, part, probs, score_grad, query_nope, grad)
    weight_parts = []
    latent_sum = None
    for h in range(2):
        columns = jnp.concatenate(
            [
                jnp.concatenate([key_grad * SCALE, value_grad], axis=1).astype(BF16)
                for key_grad, value_grad in grad_cols[h]
            ],
            axis=0,
        )
        weight_parts.append(jnp.dot(lat_t, columns, preferred_element_type=F32).astype(BF16))
        part = lax.dot_general(
            columns, w[:, h * KVW : (h + 1) * KVW], NT, preferred_element_type=F32
        )
        latent_sum = part if latent_sum is None else latent_sum + part
    return weight_parts, latent_sum


def attention_kernel(n_core, n_x, n_zl, n_y, place_ref, *refs):
    mine_ref, lat_refs, refs = refs[0], refs[1 : n_y + 1], refs[n_y + 1 :]
    q_ref, g_ref, own_w_ref, other_w_ref, keep_ref, send_ref = refs[:6]
    lg_ref, lat, bias, lat_t, total, weight = refs[6:]
    step = pl.program_id(0)
    zh, y, core = place_ref[0], place_ref[1], place_ref[2]
    rows = total.shape[0] // n_y
    tokens = rows // 2

    @pl.when(step == 0)
    def _():
        for k in range(n_y):
            start = pl.multiple_of((k * 2 + zh) * tokens, tokens)
            lat[pl.ds(start, tokens), :] = mine_ref[k * tokens : (k + 1) * tokens]
            start = pl.multiple_of((((y + n_y - k) % n_y) * 2 + 1 - zh) * tokens, tokens)
            lat[pl.ds(start, tokens), :] = lat_refs[k][...]
        key_pos = lax.broadcasted_iota(jnp.int32, (bias.shape[0], 1), 0)
        lane = lax.broadcasted_iota(jnp.int32, (1, bias.shape[1]), 1)
        block = jnp.where(lane >= 128, 2, 0) + zh
        query_pos = block * 128 + (lane & 127)
        bias[...] = jnp.where(key_pos <= query_pos, F32(0.0), F32(-1e30))
        rows_each = RANK // (n_core * n_x * n_zl)
        row = lax.broadcasted_iota(jnp.int32, (RANK, 1), 0)
        col = lax.broadcasted_iota(jnp.int32, (1, RANK), 1)
        inner = row % rows_each
        zl = (row // rows_each) % n_zl
        x = (row // (rows_each * n_zl) + place_ref[3] // n_core) % n_x
        away = row // (rows_each * n_zl * n_x)
        owner = core + away * (1 - 2 * core)
        wanted = ((x * n_zl + zl) * n_core + owner) * rows_each + inner
        pick = jnp.where(wanted == col, F32(1.0), F32(0.0)).astype(BF16)
        lat_t[...] = lax.dot_general(pick, lat[:, :RANK], NT, preferred_element_type=F32).astype(
            BF16
        )
        total[...] = jnp.zeros_like(total)

    held = step // (pl.num_programs(0) // 2) == zh

    @pl.when(held)
    def _():
        weight[...] = own_w_ref[...]

    @pl.when(jnp.logical_not(held))
    def _():
        weight[...] = other_w_ref[...]

    w = weight[...]
    kv = jnp.dot(lat[:, :RANK], w, preferred_element_type=F32).astype(BF16)
    weight_parts, latent_sum = head_pair(
        kv, lat[:, RANK : RANK + ROPE], q_ref[...], g_ref[...], w, bias[...], lat_t[...]
    )
    half = RANK // n_core
    for away, ref in enumerate((keep_ref, send_ref)):
        for h in range(2):
            part = weight_parts[h][away * half : (away + 1) * half].reshape(n_x, -1, KVW)
            ref[:, 0, :, h * KVW : (h + 1) * KVW] = part
    total[...] += latent_sum

    @pl.when(step == pl.num_programs(0) - 1)
    def _():
        lg_ref[...] = total[...].astype(BF16)


def attention(place, latents, query_grad, own_weight, other_weight, sizes):
    n_core, n_x, n_zl = sizes
    n_y = len(latents)
    q_rows, width = query_grad.shape[0], latents[0].shape[1]
    length = 2 * q_rows
    heads = 2 * own_weight.shape[1] // KVW
    steps = heads // 2
    g_blocks = heads * QW // (2 * VDIM)
    rows = RANK // (n_core * n_x)
    lat_spec = pl.BlockSpec((q_rows // n_y, width), lambda i, p: (0, 0))
    lat_block = heads * (QW + VDIM) // width
    w_spec = pl.BlockSpec((RANK, 2 * KVW), lambda i, p: (0, i % (steps // 2)))
    grad_spec = pl.BlockSpec(
        (n_x, 1, rows, 2 * KVW), lambda i, p: (0, i // (steps // 2), 0, i % (steps // 2))
    )
    grad_shape = jax.ShapeDtypeStruct((n_x, 2, rows, heads * KVW // 2), BF16)
    latent_spec = pl.BlockSpec((length, RANK), lambda i, p: (0, 0))
    latent_shape = jax.ShapeDtypeStruct((length, RANK), BF16)
    flops = heads * (3 * 2 * length * RANK * KVW + 4 * 2 * length * q_rows * 192)
    return pl.pallas_call(
        functools.partial(attention_kernel, n_core, n_x, n_zl, n_y),
        grid_spec=pltpu.PrefetchScalarGridSpec(
            num_scalar_prefetch=1,
            grid=(steps,),
            in_specs=[
                pl.BlockSpec((q_rows, width), lambda i, p: (0, lat_block)),
                *[lat_spec] * n_y,
                pl.BlockSpec((q_rows, 2 * QW), lambda i, p: (0, i)),
                pl.BlockSpec((q_rows, 2 * VDIM), lambda i, p: (0, g_blocks + i)),
                w_spec,
                w_spec,
            ],
            out_specs=[grad_spec, grad_spec, latent_spec],
            scratch_shapes=[
                pltpu.VMEM((length, width), BF16),
                pltpu.VMEM((length // 2, length // 4), F32),
                pltpu.VMEM((RANK, length), BF16),
                pltpu.VMEM((length, RANK), F32),
                pltpu.VMEM((RANK, 2 * KVW), BF16),
            ],
        ),
        out_shape=[grad_shape, grad_shape, latent_shape],
        compiler_params=pltpu.CompilerParams(
            dimension_semantics=("arbitrary",), vmem_limit_bytes=56 * 2**20
        ),
        cost_estimate=pl.CostEstimate(
            flops=flops, bytes_accessed=16 * 2**20, transcendentals=heads * length * q_rows
        ),
    )(place, query_grad, *latents, query_grad, query_grad, own_weight, other_weight)


def split_kernel(queries_ref, grads_ref, latent_ref, out_ref):
    offset = 0
    for ref in (queries_ref, grads_ref, latent_ref):
        out_ref[0, :, offset : offset + ref.shape[1]] = ref[...]
        offset += ref.shape[1]


def split_heads(queries, out_grad, packed, n_y):
    tokens = queries.shape[0]
    widths = (queries.shape[1] // n_y, out_grad.shape[1] // n_y, RANK + 2 * ROPE)
    shape = (n_y, tokens, sum(widths))
    return pl.pallas_call(
        split_kernel,
        grid=(n_y,),
        in_specs=[
            pl.BlockSpec((tokens, widths[0]), lambda i: (0, i)),
            pl.BlockSpec((tokens, widths[1]), lambda i: (0, i)),
            pl.BlockSpec((tokens, widths[2]), lambda i: (0, 0)),
        ],
        out_specs=pl.BlockSpec((1,) + shape[1:], lambda i: (i, 0, 0)),
        out_shape=jax.ShapeDtypeStruct(shape, BF16),
        cost_estimate=pl.CostEstimate(
            flops=0, bytes_accessed=4 * math.prod(shape), transcendentals=0
        ),
    )(queries, out_grad, packed)


def pack_kernel(place_ref, latent_ref, rope_ref, weight_ref, out_ref):
    tokens, rank = latent_ref.shape
    rope = rope_ref[...].astype(F32).T.astype(BF16)
    out_ref[:, :rank] = latent_ref[...]
    out_ref[:, rank : rank + 2 * ROPE] = jnp.concatenate([rope, jnp.zeros_like(rope)], axis=1)
    rows, width = weight_ref.shape
    for half in range(tokens // rows):
        columns = weight_ref[:, half * width // 2 : (half + 1) * width // 2]
        out_ref[half * rows : (half + 1) * rows, rank + 2 * ROPE :] = columns


def pack(place, latent, rope, weight, pieces):
    tokens, rank = latent.shape
    rows, width = weight.shape[0] // pieces, weight.shape[1]
    shape = (tokens, rank + 2 * ROPE + width // 2)
    return pl.pallas_call(
        pack_kernel,
        grid_spec=pltpu.PrefetchScalarGridSpec(
            num_scalar_prefetch=1,
            grid=(1,),
            in_specs=[
                pl.BlockSpec((tokens, rank), lambda i, p: (0, 0)),
                pl.BlockSpec((ROPE, tokens), lambda i, p: (0, 0)),
                pl.BlockSpec((rows, width), lambda i, p: (p[3], 0)),
            ],
            out_specs=pl.BlockSpec(shape, lambda i, p: (0, 0)),
        ),
        out_shape=jax.ShapeDtypeStruct(shape, BF16),
        cost_estimate=pl.CostEstimate(
            flops=0, bytes_accessed=4 * math.prod(shape), transcendentals=0
        ),
    )(place, latent, rope.T, weight)


def unpack_kernel(other_ref, lat_ref, weight_ref):
    width = lat_ref.shape[1]
    lat_ref[...] = other_ref[:, :width]
    count, rows, columns = weight_ref.shape
    for k in range(count):
        for half in range(2):
            part = other_ref[half * rows : (half + 1) * rows, width:]
            weight_ref[k, :, half * columns // 2 : (half + 1) * columns // 2] = part


def unpack(other, count, piece_rows):
    tokens, width = other.shape
    latent_width = RANK + 2 * ROPE
    piece = (count, piece_rows, (width - latent_width) * tokens // piece_rows)
    return pl.pallas_call(
        unpack_kernel,
        out_shape=[
            jax.ShapeDtypeStruct((tokens, latent_width), BF16),
            jax.ShapeDtypeStruct(piece, BF16),
        ],
        cost_estimate=pl.CostEstimate(
            flops=0, bytes_accessed=3 * math.prod(piece), transcendentals=0
        ),
    )(other)


def rotate(array, axis, shift):
    n = lax.axis_size(axis)
    return lax.ppermute(array, axis, [(i, (i + shift) % n) for i in range(n)])


def exchange(pieces, axes):
    return lax.all_to_all(pieces, axes, split_axis=0, concat_axis=0, tiled=True)


def add_up(pieces, dtype=BF16):
    return jnp.sum(pieces.astype(F32), axis=0).astype(dtype)


def per_device(queries, latent, key_rope, up_weight, out_grad):
    n_x, n_zl, n_core = lax.axis_size("x"), lax.axis_size("zl"), lax.axis_size("core")
    n_y, n_zh = lax.axis_size("y"), lax.axis_size("zh")
    zh, y, core = lax.axis_index("zh"), lax.axis_index("y"), lax.axis_index("core")
    mine = lax.axis_index("x") * n_core + core
    place = jnp.stack([zh, y, core, mine]).astype(jnp.int32)
    tokens = latent.shape[0]
    pieces = n_x * n_core

    packed = pack(place, latent, key_rope, up_weight, pieces)
    sent = split_heads(queries, out_grad, packed, n_y)
    query_grad = exchange(sent, "y").reshape(n_y * tokens, -1)
    latents, piece = unpack(rotate(packed, "zh", 1), pieces, RANK // pieces)
    latents = [latents] + [rotate(latents, "y", k + 1) for k in range(n_y - 1)]
    piece, query_grad = lax.optimization_barrier((piece, query_grad))
    other_weight = exchange(piece, ("x", "core")).reshape(up_weight.shape)

    sizes = (n_core, n_x, n_zl)
    keep, send, latent_part = attention(place, latents, query_grad, up_weight, other_weight, sizes)
    away = rotate(send, "core", 1)
    on_chip = [(keep[k].astype(F32) + away[k].astype(F32)).astype(BF16) for k in range(n_x)]

    arrived = exchange(latent_part.reshape(n_y, n_zh * tokens, RANK), "y")
    latent_sum = add_up(arrived, F32).reshape(n_zh, tokens, RANK)
    sent = lax.dynamic_index_in_dim(latent_sum, 1 - zh, 0, keepdims=False).astype(BF16)
    kept = lax.dynamic_index_in_dim(latent_sum, zh, 0, keepdims=False)
    sent = rotate(sent, "zh", 1)
    latent_grad = kept + sent.astype(F32)

    over_x = [on_chip[0]] + [rotate(a, "x", k + 1) for k, a in enumerate(on_chip[1:])]
    over_x = sum(a.astype(F32) for a in over_x).astype(BF16)
    over_x, _ = lax.optimization_barrier((over_x, sent))
    over_x = over_x.reshape(n_zh, n_zl, -1, over_x.shape[2]).swapaxes(0, 1)
    over_x = over_x.reshape(n_zh * n_zl, -1, over_x.shape[3])
    weight_grad = add_up(exchange(over_x, ("zl", "zh")), F32)
    return latent_grad, weight_grad * (1.0 / (n_x * n_zl * n_core))


def solution(mesh):
    replicas, parts = mesh.shape["dp"], mesh.shape["seq"]
    shape = (replicas // 16, 8, 2, parts // 2, 2)
    names = ("x", "zl", "core", "y", "zh")
    torus = Mesh(mesh.devices.reshape(shape), names)
    rows = P(names, None)
    in_specs = (rows, rows, rows, P(None, ("y", "zh")), rows)
    out_specs = (rows, P(("x", "zl", "core"), ("y", "zh")))
    return jax.shard_map(
        per_device, mesh=torus, in_specs=in_specs, out_specs=out_specs, check_vma=False
    )
```

```python
import functools
import math

import jax
import jax.numpy as jnp
from jax import lax
from jax.experimental import pallas as pl
from jax.experimental.pallas import tpu as pltpu
from jax.sharding import Mesh
from jax.sharding import PartitionSpec as P

NOPE = 128
ROPE = 64
VDIM = 128
QW = NOPE + ROPE
KVW = NOPE + VDIM
RANK = 512
SCALE = QW ** (-0.5)
BF16 = jnp.bfloat16
F32 = jnp.float32
NT = (((1,), (1,)), ((), ()))


def head_pair(kv, rope, q2, g2, w, bias, lat_t):
    half = kv.shape[0] // 2
    rows_each = half // 2
    grad_cols = [[[None, None], [None, None]] for _ in range(2)]

    def products(h, part):
        n_keys = half * (part + 1)
        rows = slice(part * rows_each, (part + 1) * rows_each)
        keys = jnp.concatenate([kv[:n_keys, h * KVW : h * KVW + NOPE], rope[:n_keys]], axis=1)
        values = kv[:n_keys, h * KVW + NOPE : (h + 1) * KVW]
        query = q2[rows, h * QW : (h + 1) * QW]
        grad = g2[rows, h * VDIM : (h + 1) * VDIM]
        scores = lax.dot_general(keys, query, NT, preferred_element_type=F32)
        prob_grad = lax.dot_general(values, grad, NT, preferred_element_type=F32)
        return scores, prob_grad, query[:, :NOPE], grad

    def softmax(part, scores, prob_grad):
        if part == 0:
            scores = scores + bias
        else:
            scores = jnp.concatenate([scores[:half], scores[half:] + bias], axis=0)
        row_max = jnp.max(scores, axis=0, keepdims=True)
        expo = jnp.exp2((scores - row_max) * (SCALE * math.log2(math.e)))
        probs = expo * (1.0 / jnp.sum(expo, axis=0, keepdims=True))
        row_dot = jnp.sum(probs * prob_grad, axis=0, keepdims=True)
        return probs.astype(BF16), (probs * (prob_grad - row_dot)).astype(BF16)

    def accumulate(h, part, probs, score_grad, query_nope, grad):
        for block in range(part + 1):
            cut = slice(block * half, (block + 1) * half)
            for which, (left, right) in enumerate(((score_grad, query_nope), (probs, grad))):
                product = jnp.dot(left[cut], right, preferred_element_type=F32)
                before = grad_cols[h][block][which]
                grad_cols[h][block][which] = product if before is None else before + product

    units = [(h, part) for h in range(2) for part in (1, 0)]
    ready = products(*units[0])
    for n, (h, part) in enumerate(units):
        scores, prob_grad, query_nope, grad = ready
        if n + 1 < len(units):
            ready = products(*units[n + 1])
        probs, score_grad = softmax(part, scores, prob_grad)
        accumulate(h, part, probs, score_grad, query_nope, grad)
    weight_parts = []
    latent_sum = None
    for h in range(2):
        columns = jnp.concatenate(
            [
                jnp.concatenate([key_grad * SCALE, value_grad], axis=1).astype(BF16)
                for key_grad, value_grad in grad_cols[h]
            ],
            axis=0,
        )
        weight_parts.append(jnp.dot(lat_t, columns, preferred_element_type=F32).astype(BF16))
        part = lax.dot_general(
            columns, w[:, h * KVW : (h + 1) * KVW], NT, preferred_element_type=F32
        )
        latent_sum = part if latent_sum is None else latent_sum + part
    return weight_parts, latent_sum


def attention_kernel(n_core, n_x, n_zl, n_y, place_ref, *refs):
    mine_ref, lat_refs, refs = refs[0], refs[1 : n_y + 1], refs[n_y + 1 :]
    q_ref, g_ref, own_w_ref, other_w_ref, keep_ref, send_ref = refs[:6]
    lg_ref, lat, bias, lat_t, total, weight = refs[6:]
    step = pl.program_id(0)
    zh, y, core = place_ref[0], place_ref[1], place_ref[2]
    rows = total.shape[0] // n_y
    tokens = rows // 2

    @pl.when(step == 0)
    def _():
        for k in range(n_y):
            start = pl.multiple_of((k * 2 + zh) * tokens, tokens)
            lat[pl.ds(start, tokens), :] = mine_ref[k * tokens : (k + 1) * tokens]
            start = pl.multiple_of((((y + n_y - k) % n_y) * 2 + 1 - zh) * tokens, tokens)
            lat[pl.ds(start, tokens), :] = lat_refs[k][...]
        key_pos = lax.broadcasted_iota(jnp.int32, (bias.shape[0], 1), 0)
        lane = lax.broadcasted_iota(jnp.int32, (1, bias.shape[1]), 1)
        block = jnp.where(lane >= 128, 2, 0) + zh
        query_pos = block * 128 + (lane & 127)
        bias[...] = jnp.where(key_pos <= query_pos, F32(0.0), F32(-1e30))
        rows_each = RANK // (n_core * n_x * n_zl)
        row = lax.broadcasted_iota(jnp.int32, (RANK, 1), 0)
        col = lax.broadcasted_iota(jnp.int32, (1, RANK), 1)
        inner = row % rows_each
        zl = (row // rows_each) % n_zl
        x = (row // (rows_each * n_zl) + place_ref[3] // n_core) % n_x
        away = row // (rows_each * n_zl * n_x)
        owner = core + away * (1 - 2 * core)
        wanted = ((x * n_zl + zl) * n_core + owner) * rows_each + inner
        pick = jnp.where(wanted == col, F32(1.0), F32(0.0)).astype(BF16)
        lat_t[...] = lax.dot_general(pick, lat[:, :RANK], NT, preferred_element_type=F32).astype(
            BF16
        )
        total[...] = jnp.zeros_like(total)

    held = step // (pl.num_programs(0) // 2) == zh

    @pl.when(held)
    def _():
        weight[...] = own_w_ref[...]

    @pl.when(jnp.logical_not(held))
    def _():
        weight[...] = other_w_ref[...]

    w = weight[...]
    kv = jnp.dot(lat[:, :RANK], w, preferred_element_type=F32).astype(BF16)
    weight_parts, latent_sum = head_pair(
        kv, lat[:, RANK : RANK + ROPE], q_ref[...], g_ref[...], w, bias[...], lat_t[...]
    )
    half = RANK // n_core
    for away, ref in enumerate((keep_ref, send_ref)):
        for h in range(2):
            part = weight_parts[h][away * half : (away + 1) * half].reshape(n_x, -1, KVW)
            ref[:, 0, :, h * KVW : (h + 1) * KVW] = part
    total[...] += latent_sum

    @pl.when(step == pl.num_programs(0) - 1)
    def _():
        lg_ref[...] = total[...].astype(BF16)


def attention(place, latents, query_grad, own_weight, other_weight, sizes):
    n_core, n_x, n_zl = sizes
    n_y = len(latents)
    q_rows, width = query_grad.shape[0], latents[0].shape[1]
    length = 2 * q_rows
    heads = 2 * own_weight.shape[1] // KVW
    steps = heads // 2
    g_blocks = heads * QW // (2 * VDIM)
    rows = RANK // (n_core * n_x)
    lat_spec = pl.BlockSpec((q_rows // n_y, width), lambda i, p: (0, 0))
    lat_block = heads * (QW + VDIM) // width
    w_spec = pl.BlockSpec((RANK, 2 * KVW), lambda i, p: (0, i % (steps // 2)))
    grad_spec = pl.BlockSpec(
        (n_x, 1, rows, 2 * KVW), lambda i, p: (0, i // (steps // 2), 0, i % (steps // 2))
    )
    grad_shape = jax.ShapeDtypeStruct((n_x, 2, rows, heads * KVW // 2), BF16)
    latent_spec = pl.BlockSpec((length, RANK), lambda i, p: (0, 0))
    latent_shape = jax.ShapeDtypeStruct((length, RANK), BF16)
    flops = heads * (3 * 2 * length * RANK * KVW + 4 * 2 * length * q_rows * 192)
    return pl.pallas_call(
        functools.partial(attention_kernel, n_core, n_x, n_zl, n_y),
        grid_spec=pltpu.PrefetchScalarGridSpec(
            num_scalar_prefetch=1,
            grid=(steps,),
            in_specs=[
                pl.BlockSpec((q_rows, width), lambda i, p: (0, lat_block)),
                *[lat_spec] * n_y,
                pl.BlockSpec((q_rows, 2 * QW), lambda i, p: (0, i)),
                pl.BlockSpec((q_rows, 2 * VDIM), lambda i, p: (0, g_blocks + i)),
                w_spec,
                w_spec,
            ],
            out_specs=[grad_spec, grad_spec, latent_spec],
            scratch_shapes=[
                pltpu.VMEM((length, width), BF16),
                pltpu.VMEM((length // 2, length // 4), F32),
                pltpu.VMEM((RANK, length), BF16),
                pltpu.VMEM((length, RANK), F32),
                pltpu.VMEM((RANK, 2 * KVW), BF16),
            ],
        ),
        out_shape=[grad_shape, grad_shape, latent_shape],
        compiler_params=pltpu.CompilerParams(
            dimension_semantics=("arbitrary",), vmem_limit_bytes=56 * 2**20
        ),
        cost_estimate=pl.CostEstimate(
            flops=flops, bytes_accessed=16 * 2**20, transcendentals=heads * length * q_rows
        ),
    )(place, query_grad, *latents, query_grad, query_grad, own_weight, other_weight)


def latent_columns(latent_ref, rope_ref):
    rope = rope_ref[...].astype(F32).T.astype(BF16)
    return jnp.concatenate([latent_ref[...], rope, jnp.zeros_like(rope)], axis=1)


def split_kernel(queries_ref, grads_ref, latent_ref, rope_ref, out_ref):
    q_width, g_width = queries_ref.shape[1], grads_ref.shape[1]
    out_ref[0, :, :q_width] = queries_ref[...]
    out_ref[0, :, q_width : q_width + g_width] = grads_ref[...]
    out_ref[0, :, q_width + g_width :] = latent_columns(latent_ref, rope_ref)


def split_heads(queries, out_grad, latent, rope, n_y):
    tokens, rank = latent.shape
    widths = (queries.shape[1] // n_y, out_grad.shape[1] // n_y)
    shape = (n_y, tokens, sum(widths) + rank + 2 * ROPE)
    return pl.pallas_call(
        split_kernel,
        grid=(n_y,),
        in_specs=[
            pl.BlockSpec((tokens, widths[0]), lambda i: (0, i)),
            pl.BlockSpec((tokens, widths[1]), lambda i: (0, i)),
            pl.BlockSpec((tokens, rank), lambda i: (0, 0)),
            pl.BlockSpec((ROPE, tokens), lambda i: (0, 0)),
        ],
        out_specs=pl.BlockSpec((1,) + shape[1:], lambda i: (i, 0, 0)),
        out_shape=jax.ShapeDtypeStruct(shape, BF16),
        cost_estimate=pl.CostEstimate(
            flops=0, bytes_accessed=4 * math.prod(shape), transcendentals=0
        ),
    )(queries, out_grad, latent, rope.T)


def pack_kernel(place_ref, latent_ref, rope_ref, weight_ref, out_ref):
    tokens, rank = latent_ref.shape
    out_ref[:, : rank + 2 * ROPE] = latent_columns(latent_ref, rope_ref)
    rows, width = weight_ref.shape
    for half in range(tokens // rows):
        columns = weight_ref[:, half * width // 2 : (half + 1) * width // 2]
        out_ref[half * rows : (half + 1) * rows, rank + 2 * ROPE :] = columns


def pack(place, latent, rope, weight, pieces):
    tokens, rank = latent.shape
    rows, width = weight.shape[0] // pieces, weight.shape[1]
    shape = (tokens, rank + 2 * ROPE + width // 2)
    return pl.pallas_call(
        pack_kernel,
        grid_spec=pltpu.PrefetchScalarGridSpec(
            num_scalar_prefetch=1,
            grid=(1,),
            in_specs=[
                pl.BlockSpec((tokens, rank), lambda i, p: (0, 0)),
                pl.BlockSpec((ROPE, tokens), lambda i, p: (0, 0)),
                pl.BlockSpec((rows, width), lambda i, p: (p[3], 0)),
            ],
            out_specs=pl.BlockSpec(shape, lambda i, p: (0, 0)),
        ),
        out_shape=jax.ShapeDtypeStruct(shape, BF16),
        cost_estimate=pl.CostEstimate(
            flops=0, bytes_accessed=4 * math.prod(shape), transcendentals=0
        ),
    )(place, latent, rope.T, weight)


def unpack_kernel(other_ref, lat_ref, weight_ref):
    width = lat_ref.shape[1]
    lat_ref[...] = other_ref[:, :width]
    count, rows, columns = weight_ref.shape
    for k in range(count):
        for half in range(2):
            part = other_ref[half * rows : (half + 1) * rows, width:]
            weight_ref[k, :, half * columns // 2 : (half + 1) * columns // 2] = part


def unpack(other, count, piece_rows):
    tokens, width = other.shape
    latent_width = RANK + 2 * ROPE
    piece = (count, piece_rows, (width - latent_width) * tokens // piece_rows)
    return pl.pallas_call(
        unpack_kernel,
        out_shape=[
            jax.ShapeDtypeStruct((tokens, latent_width), BF16),
            jax.ShapeDtypeStruct(piece, BF16),
        ],
        cost_estimate=pl.CostEstimate(
            flops=0, bytes_accessed=3 * math.prod(piece), transcendentals=0
        ),
    )(other)


def rotate(array, axis, shift):
    n = lax.axis_size(axis)
    return lax.ppermute(array, axis, [(i, (i + shift) % n) for i in range(n)])


def exchange(pieces, axes):
    return lax.all_to_all(pieces, axes, split_axis=0, concat_axis=0, tiled=True)


def add_up(pieces, dtype=BF16):
    return jnp.sum(pieces.astype(F32), axis=0).astype(dtype)


def per_device(queries, latent, key_rope, up_weight, out_grad):
    n_x, n_zl, n_core = lax.axis_size("x"), lax.axis_size("zl"), lax.axis_size("core")
    n_y, n_zh = lax.axis_size("y"), lax.axis_size("zh")
    zh, y, core = lax.axis_index("zh"), lax.axis_index("y"), lax.axis_index("core")
    mine = lax.axis_index("x") * n_core + core
    place = jnp.stack([zh, y, core, mine]).astype(jnp.int32)
    tokens = latent.shape[0]
    pieces = n_x * n_core

    packed = pack(place, latent, key_rope, up_weight, pieces)
    sent = split_heads(queries, out_grad, latent, key_rope, n_y)
    query_grad = exchange(sent, "y").reshape(n_y * tokens, -1)
    latents, piece = unpack(rotate(packed, "zh", 1), pieces, RANK // pieces)
    latents = [latents] + [rotate(latents, "y", k + 1) for k in range(n_y - 1)]
    piece, query_grad = lax.optimization_barrier((piece, query_grad))
    other_weight = exchange(piece, ("x", "core")).reshape(up_weight.shape)

    sizes = (n_core, n_x, n_zl)
    keep, send, latent_part = attention(place, latents, query_grad, up_weight, other_weight, sizes)
    away = rotate(send, "core", 1)
    on_chip = [(keep[k].astype(F32) + away[k].astype(F32)).astype(BF16) for k in range(n_x)]

    arrived = exchange(latent_part.reshape(n_y, n_zh * tokens, RANK), "y")
    latent_sum = add_up(arrived, F32).reshape(n_zh, tokens, RANK)
    sent = lax.dynamic_index_in_dim(latent_sum, 1 - zh, 0, keepdims=False).astype(BF16)
    kept = lax.dynamic_index_in_dim(latent_sum, zh, 0, keepdims=False)
    sent = rotate(sent, "zh", 1)
    over_x = [on_chip[0]] + [rotate(a, "x", k + 1) for k, a in enumerate(on_chip[1:])]
    over_x = sum(a.astype(F32) for a in over_x).astype(BF16)
    rows = over_x.shape[1] // n_zl
    pieces = over_x.reshape(n_zh, n_zl, rows, -1).swapaxes(0, 1)
    over_zl = add_up(exchange(pieces, "zl"), F32)
    over_zl, sent = lax.optimization_barrier((over_zl, sent))
    latent_grad = kept + sent.astype(F32)
    own = lax.dynamic_index_in_dim(over_zl, zh, 0, keepdims=False)
    other = lax.dynamic_index_in_dim(over_zl, 1 - zh, 0, keepdims=False)
    weight_grad = own + rotate(other, "zh", 1)
    return latent_grad, weight_grad * (1.0 / (n_x * n_zl * n_core))


def solution(mesh):
    replicas, parts = mesh.shape["dp"], mesh.shape["seq"]
    shape = (replicas // 16, 8, 2, parts // 2, 2)
    names = ("x", "zl", "core", "y", "zh")
    torus = Mesh(mesh.devices.reshape(shape), names)
    rows = P(names, None)
    in_specs = (rows, rows, rows, P(None, ("y", "zh")), rows)
    out_specs = (rows, P(("x", "zl", "core"), ("y", "zh")))
    return jax.shard_map(
        per_device, mesh=torus, in_specs=in_specs, out_specs=out_specs, check_vma=False
    )
```

```python
import functools
import math

import jax
import jax.numpy as jnp
from jax import lax
from jax.experimental import pallas as pl
from jax.experimental.pallas import tpu as pltpu
from jax.sharding import Mesh
from jax.sharding import PartitionSpec as P

NOPE = 128
ROPE = 64
VDIM = 128
QW = NOPE + ROPE
KVW = NOPE + VDIM
RANK = 512
SCALE = QW ** (-0.5)
BF16 = jnp.bfloat16
F32 = jnp.float32
ZL = ("zm", "zn")
HOLDERS = ("x", "zn", "core")
NT = (((1,), (1,)), ((), ()))


def head_pair(kv, rope, q2, g2, w, bias, lat_t):
    half = kv.shape[0] // 2
    rows_each = half // 2
    grad_cols = [[[None, None], [None, None]] for _ in range(2)]

    def products(h, part):
        n_keys = half * (part + 1)
        rows = slice(part * rows_each, (part + 1) * rows_each)
        keys = jnp.concatenate([kv[:n_keys, h * KVW : h * KVW + NOPE], rope[:n_keys]], axis=1)
        values = kv[:n_keys, h * KVW + NOPE : (h + 1) * KVW]
        query = q2[rows, h * QW : (h + 1) * QW]
        grad = g2[rows, h * VDIM : (h + 1) * VDIM]
        scores = lax.dot_general(keys, query, NT, preferred_element_type=F32)
        prob_grad = lax.dot_general(values, grad, NT, preferred_element_type=F32)
        return scores, prob_grad, query[:, :NOPE], grad

    def softmax(part, scores, prob_grad):
        if part == 0:
            scores = scores + bias
        else:
            scores = jnp.concatenate([scores[:half], scores[half:] + bias], axis=0)
        row_max = jnp.max(scores, axis=0, keepdims=True)
        expo = jnp.exp2((scores - row_max) * (SCALE * math.log2(math.e)))
        probs = expo * (1.0 / jnp.sum(expo, axis=0, keepdims=True))
        row_dot = jnp.sum(probs * prob_grad, axis=0, keepdims=True)
        return probs.astype(BF16), (probs * (prob_grad - row_dot)).astype(BF16)

    def accumulate(h, part, probs, score_grad, query_nope, grad):
        for block in range(part + 1):
            cut = slice(block * half, (block + 1) * half)
            for which, (left, right) in enumerate(((score_grad, query_nope), (probs, grad))):
                product = jnp.dot(left[cut], right, preferred_element_type=F32)
                before = grad_cols[h][block][which]
                grad_cols[h][block][which] = product if before is None else before + product

    units = [(h, part) for h in range(2) for part in (1, 0)]
    ready = products(*units[0])
    for n, (h, part) in enumerate(units):
        scores, prob_grad, query_nope, grad = ready
        if n + 1 < len(units):
            ready = products(*units[n + 1])
        probs, score_grad = softmax(part, scores, prob_grad)
        accumulate(h, part, probs, score_grad, query_nope, grad)
    weight_parts = []
    latent_sum = None
    for h in range(2):
        columns = jnp.concatenate(
            [
                jnp.concatenate([key_grad * SCALE, value_grad], axis=1).astype(BF16)
                for key_grad, value_grad in grad_cols[h]
            ],
            axis=0,
        )
        weight_parts.append(jnp.dot(lat_t, columns, preferred_element_type=F32).astype(BF16))
        part = lax.dot_general(
            columns, w[:, h * KVW : (h + 1) * KVW], NT, preferred_element_type=F32
        )
        latent_sum = part if latent_sum is None else latent_sum + part
    return weight_parts, latent_sum


def attention_kernel(n_core, n_x, n_zl, n_y, place_ref, *refs):
    mine_ref, lat_refs, refs = refs[0], refs[1 : n_y + 1], refs[n_y + 1 :]
    q_ref, g_ref, own_w_ref, other_w_ref, keep_ref, send_ref = refs[:6]
    lg_ref, lat, bias, lat_t, total, weight = refs[6:]
    step = pl.program_id(0)
    zh, y, core = place_ref[0], place_ref[1], place_ref[2]
    rows = total.shape[0] // n_y
    tokens = rows // 2

    @pl.when(step == 0)
    def _():
        for k in range(n_y):
            start = pl.multiple_of((k * 2 + zh) * tokens, tokens)
            lat[pl.ds(start, tokens), :] = mine_ref[k * tokens : (k + 1) * tokens]
            start = pl.multiple_of((((y + n_y - k) % n_y) * 2 + 1 - zh) * tokens, tokens)
            lat[pl.ds(start, tokens), :] = lat_refs[k][...]
        key_pos = lax.broadcasted_iota(jnp.int32, (bias.shape[0], 1), 0)
        lane = lax.broadcasted_iota(jnp.int32, (1, bias.shape[1]), 1)
        block = jnp.where(lane >= 128, 2, 0) + zh
        query_pos = block * 128 + (lane & 127)
        bias[...] = jnp.where(key_pos <= query_pos, F32(0.0), F32(-1e30))
        rows_each = RANK // (n_core * n_x * n_zl)
        row = lax.broadcasted_iota(jnp.int32, (RANK, 1), 0)
        col = lax.broadcasted_iota(jnp.int32, (1, RANK), 1)
        inner = row % rows_each
        zl = (row // rows_each) % n_zl
        x = (row // (rows_each * n_zl) + place_ref[4]) % n_x
        away = row // (rows_each * n_zl * n_x)
        owner = core + away * (1 - 2 * core)
        wanted = ((x * n_zl + zl) * n_core + owner) * rows_each + inner
        pick = jnp.where(wanted == col, F32(1.0), F32(0.0)).astype(BF16)
        lat_t[...] = lax.dot_general(pick, lat[:, :RANK], NT, preferred_element_type=F32).astype(
            BF16
        )
        total[...] = jnp.zeros_like(total)

    held = step // (pl.num_programs(0) // 2) == zh

    @pl.when(held)
    def _():
        weight[...] = own_w_ref[...]

    @pl.when(jnp.logical_not(held))
    def _():
        weight[...] = other_w_ref[...]

    w = weight[...]
    kv = jnp.dot(lat[:, :RANK], w, preferred_element_type=F32).astype(BF16)
    weight_parts, latent_sum = head_pair(
        kv, lat[:, RANK : RANK + ROPE], q_ref[...], g_ref[...], w, bias[...], lat_t[...]
    )
    half = RANK // n_core
    for away, ref in enumerate((keep_ref, send_ref)):
        for h in range(2):
            part = weight_parts[h][away * half : (away + 1) * half].reshape(n_x, -1, KVW)
            ref[:, 0, :, h * KVW : (h + 1) * KVW] = part
    total[...] += latent_sum

    @pl.when(step == pl.num_programs(0) - 1)
    def _():
        lg_ref[...] = total[...].astype(BF16)


def attention(place, latents, query_grad, own_weight, other_weight, sizes):
    n_core, n_x, n_zl = sizes
    n_y = len(latents)
    q_rows, width = query_grad.shape[0], latents[0].shape[1]
    length = 2 * q_rows
    heads = 2 * own_weight.shape[1] // KVW
    steps = heads // 2
    g_blocks = heads * QW // (2 * VDIM)
    rows = RANK // (n_core * n_x)
    lat_spec = pl.BlockSpec((q_rows // n_y, width), lambda i, p: (0, 0))
    lat_block = heads * (QW + VDIM) // width
    w_spec = pl.BlockSpec((RANK, 2 * KVW), lambda i, p: (0, i % (steps // 2)))
    grad_spec = pl.BlockSpec(
        (n_x, 1, rows, 2 * KVW), lambda i, p: (0, i // (steps // 2), 0, i % (steps // 2))
    )
    grad_shape = jax.ShapeDtypeStruct((n_x, 2, rows, heads * KVW // 2), BF16)
    latent_spec = pl.BlockSpec((length, RANK), lambda i, p: (0, 0))
    latent_shape = jax.ShapeDtypeStruct((length, RANK), BF16)
    flops = heads * (3 * 2 * length * RANK * KVW + 4 * 2 * length * q_rows * 192)
    return pl.pallas_call(
        functools.partial(attention_kernel, n_core, n_x, n_zl, n_y),
        grid_spec=pltpu.PrefetchScalarGridSpec(
            num_scalar_prefetch=1,
            grid=(steps,),
            in_specs=[
                pl.BlockSpec((q_rows, width), lambda i, p: (0, lat_block)),
                *[lat_spec] * n_y,
                pl.BlockSpec((q_rows, 2 * QW), lambda i, p: (0, i)),
                pl.BlockSpec((q_rows, 2 * VDIM), lambda i, p: (0, g_blocks + i)),
                w_spec,
                w_spec,
            ],
            out_specs=[grad_spec, grad_spec, latent_spec],
            scratch_shapes=[
                pltpu.VMEM((length, width), BF16),
                pltpu.VMEM((length // 2, length // 4), F32),
                pltpu.VMEM((RANK, length), BF16),
                pltpu.VMEM((length, RANK), F32),
                pltpu.VMEM((RANK, 2 * KVW), BF16),
            ],
        ),
        out_shape=[grad_shape, grad_shape, latent_shape],
        compiler_params=pltpu.CompilerParams(
            dimension_semantics=("arbitrary",), vmem_limit_bytes=56 * 2**20
        ),
        cost_estimate=pl.CostEstimate(
            flops=flops, bytes_accessed=16 * 2**20, transcendentals=heads * length * q_rows
        ),
    )(place, query_grad, *latents, query_grad, query_grad, own_weight, other_weight)


def latent_columns(latent_ref, rope_ref):
    rope = rope_ref[...].astype(F32).T.astype(BF16)
    return jnp.concatenate([latent_ref[...], rope, jnp.zeros_like(rope)], axis=1)


def split_kernel(queries_ref, grads_ref, latent_ref, rope_ref, out_ref):
    q_width, g_width = queries_ref.shape[1], grads_ref.shape[1]
    out_ref[0, :, :q_width] = queries_ref[...]
    out_ref[0, :, q_width : q_width + g_width] = grads_ref[...]
    out_ref[0, :, q_width + g_width :] = latent_columns(latent_ref, rope_ref)


def split_heads(queries, out_grad, latent, rope, n_y):
    tokens, rank = latent.shape
    widths = (queries.shape[1] // n_y, out_grad.shape[1] // n_y)
    shape = (n_y, tokens, sum(widths) + rank + 2 * ROPE)
    return pl.pallas_call(
        split_kernel,
        grid=(n_y,),
        in_specs=[
            pl.BlockSpec((tokens, widths[0]), lambda i: (0, i)),
            pl.BlockSpec((tokens, widths[1]), lambda i: (0, i)),
            pl.BlockSpec((tokens, rank), lambda i: (0, 0)),
            pl.BlockSpec((ROPE, tokens), lambda i: (0, 0)),
        ],
        out_specs=pl.BlockSpec((1,) + shape[1:], lambda i: (i, 0, 0)),
        out_shape=jax.ShapeDtypeStruct(shape, BF16),
        cost_estimate=pl.CostEstimate(
            flops=0, bytes_accessed=4 * math.prod(shape), transcendentals=0
        ),
    )(queries, out_grad, latent, rope.T)


def pack_kernel(place_ref, latent_ref, rope_ref, weight_ref, out_ref):
    tokens, rank = latent_ref.shape
    out_ref[:, : rank + 2 * ROPE] = latent_columns(latent_ref, rope_ref)
    rows, width = weight_ref.shape
    width = width * rows // tokens
    for k in range(tokens // rows):
        columns = weight_ref[:, k * width : (k + 1) * width]
        out_ref[k * rows : (k + 1) * rows, rank + 2 * ROPE :] = columns


def pack(place, latent, rope, weight, pieces):
    tokens, rank = latent.shape
    rows, width = weight.shape[0] // pieces, weight.shape[1]
    shape = (tokens, rank + 2 * ROPE + width * rows // tokens)
    return pl.pallas_call(
        pack_kernel,
        grid_spec=pltpu.PrefetchScalarGridSpec(
            num_scalar_prefetch=1,
            grid=(1,),
            in_specs=[
                pl.BlockSpec((tokens, rank), lambda i, p: (0, 0)),
                pl.BlockSpec((ROPE, tokens), lambda i, p: (0, 0)),
                pl.BlockSpec((rows, width), lambda i, p: (p[3], 0)),
            ],
            out_specs=pl.BlockSpec(shape, lambda i, p: (0, 0)),
        ),
        out_shape=jax.ShapeDtypeStruct(shape, BF16),
        cost_estimate=pl.CostEstimate(
            flops=0, bytes_accessed=4 * math.prod(shape), transcendentals=0
        ),
    )(place, latent, rope.T, weight)


def unpack_kernel(other_ref, lat_ref, weight_ref):
    width = lat_ref.shape[1]
    lat_ref[...] = other_ref[:, :width]
    count, rows, columns = weight_ref.shape
    blocks = lat_ref.shape[0] // rows
    columns = columns // blocks
    for k in range(count):
        for block in range(blocks):
            part = other_ref[block * rows : (block + 1) * rows, width:]
            weight_ref[k, :, block * columns : (block + 1) * columns] = part


def unpack(other, count, piece_rows):
    tokens, width = other.shape
    latent_width = RANK + 2 * ROPE
    piece = (count, piece_rows, (width - latent_width) * tokens // piece_rows)
    return pl.pallas_call(
        unpack_kernel,
        out_shape=[
            jax.ShapeDtypeStruct((tokens, latent_width), BF16),
            jax.ShapeDtypeStruct(piece, BF16),
        ],
        cost_estimate=pl.CostEstimate(
            flops=0, bytes_accessed=3 * math.prod(piece), transcendentals=0
        ),
    )(other)


def rotate(array, axis, shift):
    n = lax.axis_size(axis)
    return lax.ppermute(array, axis, [(i, (i + shift) % n) for i in range(n)])


def exchange(pieces, axes):
    return lax.all_to_all(pieces, axes, split_axis=0, concat_axis=0, tiled=True)


def add_up(pieces, dtype=BF16):
    return jnp.sum(pieces.astype(F32), axis=0).astype(dtype)


def per_device(queries, latent, key_rope, up_weight, out_grad):
    n_x, n_zl, n_core = lax.axis_size("x"), lax.axis_size(ZL), lax.axis_size("core")
    n_y, n_zh = lax.axis_size("y"), lax.axis_size("zh")
    zh, y, core = lax.axis_index("zh"), lax.axis_index("y"), lax.axis_index("core")
    mine = lax.axis_index(HOLDERS)
    place = jnp.stack([zh, y, core, mine, lax.axis_index("x")]).astype(jnp.int32)
    tokens = latent.shape[0]
    pieces = lax.axis_size(HOLDERS)

    packed = pack(place, latent, key_rope, up_weight, pieces)
    sent = split_heads(queries, out_grad, latent, key_rope, n_y)
    query_grad = exchange(sent, "y").reshape(n_y * tokens, -1)
    latents, piece = unpack(rotate(packed, "zh", 1), pieces, RANK // pieces)
    latents = [latents] + [rotate(latents, "y", k + 1) for k in range(n_y - 1)]
    piece, query_grad = lax.optimization_barrier((piece, query_grad))
    other_weight = exchange(piece, HOLDERS).reshape(up_weight.shape)

    sizes = (n_core, n_x, n_zl)
    keep, send, latent_part = attention(place, latents, query_grad, up_weight, other_weight, sizes)
    away = rotate(send, "core", 1)
    on_chip = [(keep[k].astype(F32) + away[k].astype(F32)).astype(BF16) for k in range(n_x)]

    arrived = exchange(latent_part.reshape(n_y, n_zh * tokens, RANK), "y")
    latent_sum = add_up(arrived, F32).reshape(n_zh, tokens, RANK)
    sent = lax.dynamic_index_in_dim(latent_sum, 1 - zh, 0, keepdims=False).astype(BF16)
    kept = lax.dynamic_index_in_dim(latent_sum, zh, 0, keepdims=False)
    sent = rotate(sent, "zh", 1)
    over_x = [on_chip[0]] + [rotate(a, "x", k + 1) for k, a in enumerate(on_chip[1:])]
    over_x = sum(a.astype(F32) for a in over_x).astype(BF16)
    rows = over_x.shape[1] // n_zl
    pieces = over_x.reshape(n_zh, n_zl, rows, -1).swapaxes(0, 1)
    over_zl = add_up(exchange(pieces, ZL), F32)
    latent_grad = kept + sent.astype(F32)
    own = lax.dynamic_index_in_dim(over_zl, zh, 0, keepdims=False)
    other = lax.dynamic_index_in_dim(over_zl, 1 - zh, 0, keepdims=False)
    weight_grad = own + rotate(other, "zh", 1)
    return latent_grad, weight_grad * (1.0 / (n_x * n_zl * n_core))


def solution(mesh):
    replicas, parts = mesh.shape["dp"], mesh.shape["seq"]
    shape = (replicas // 16, 4, 2, 2, parts // 2, 2)
    names = ("x", *ZL, "core", "y", "zh")
    torus = Mesh(mesh.devices.reshape(shape), names)
    rows = P(names, None)
    in_specs = (rows, rows, rows, P(None, ("y", "zh")), rows)
    out_specs = (rows, P(("x", *ZL, "core"), ("y", "zh")))
    return jax.shard_map(
        per_device, mesh=torus, in_specs=in_specs, out_specs=out_specs, check_vma=False
    )
```

```python
import functools
import math

import jax
import jax.numpy as jnp
from jax import lax
from jax.experimental import pallas as pl
from jax.experimental.pallas import tpu as pltpu
from jax.sharding import Mesh
from jax.sharding import PartitionSpec as P

NOPE = 128
ROPE = 64
VDIM = 128
QW = NOPE + ROPE
KVW = NOPE + VDIM
RANK = 512
SCALE = QW ** (-0.5)
BF16 = jnp.bfloat16
F32 = jnp.float32
ZL = ("zm", "zn")
HOLDERS = ("x", "zn", "core")
NT = (((1,), (1,)), ((), ()))


def head_pair(kv, rope, q2, g2, w, bias, lat_t):
    half = kv.shape[0] // 2
    rows_each = half // 2
    grad_cols = [[[None, None], [None, None]] for _ in range(2)]

    def products(h, part):
        rows = slice(part * rows_each, (part + 1) * rows_each)
        query = q2[rows, h * QW : (h + 1) * QW]
        grad = g2[rows, h * VDIM : (h + 1) * VDIM]
        pairs = []
        for block in range(part + 1):
            cut = slice(block * half, (block + 1) * half)
            keys = jnp.concatenate([kv[cut, h * KVW : h * KVW + NOPE], rope[cut]], axis=1)
            values = kv[cut, h * KVW + NOPE : (h + 1) * KVW]
            scores = lax.dot_general(keys, query, NT, preferred_element_type=F32)
            if block == part:
                scores = scores + bias
            prob_grad = lax.dot_general(values, grad, NT, preferred_element_type=F32)
            pairs.append((scores, prob_grad))
        return pairs, query[:, :NOPE], grad

    def over_keys(reduce, combine, blocks):
        return functools.reduce(combine, [reduce(b, axis=0, keepdims=True) for b in blocks])

    def softmax(pairs):
        row_max = over_keys(jnp.max, jnp.maximum, [scores for scores, _ in pairs])
        expo = [
            jnp.exp2((scores - row_max) * (SCALE * math.log2(math.e))) for scores, _ in pairs
        ]
        inverse = 1.0 / over_keys(jnp.sum, jnp.add, expo)
        probs = [e * inverse for e in expo]
        row_dot = over_keys(jnp.sum, jnp.add, [p * g for p, (_, g) in zip(probs, pairs)])
        return [(p.astype(BF16), (p * (g - row_dot)).astype(BF16)) for p, (_, g) in zip(probs, pairs)]

    def accumulate(h, blocks, query_nope, grad):
        for block, (probs, score_grad) in enumerate(blocks):
            for which, (left, right) in enumerate(((score_grad, query_nope), (probs, grad))):
                product = jnp.dot(left, right, preferred_element_type=F32)
                before = grad_cols[h][block][which]
                grad_cols[h][block][which] = product if before is None else before + product

    units = [(h, part) for h in range(2) for part in (1, 0)]
    ready = products(*units[0])
    for n, (h, part) in enumerate(units):
        pairs, query_nope, grad = ready
        if n + 1 < len(units):
            ready = products(*units[n + 1])
        accumulate(h, softmax(pairs), query_nope, grad)
    weight_parts = []
    latent_sum = None
    for h in range(2):
        columns = jnp.concatenate(
            [
                jnp.concatenate([key_grad * SCALE, value_grad], axis=1).astype(BF16)
                for key_grad, value_grad in grad_cols[h]
            ],
            axis=0,
        )
        weight_parts.append(jnp.dot(lat_t, columns, preferred_element_type=F32).astype(BF16))
        part = lax.dot_general(
            columns, w[:, h * KVW : (h + 1) * KVW], NT, preferred_element_type=F32
        )
        latent_sum = part if latent_sum is None else latent_sum + part
    return weight_parts, latent_sum


def attention_kernel(n_core, n_x, n_zl, n_y, place_ref, *refs):
    mine_ref, lat_refs, refs = refs[0], refs[1 : n_y + 1], refs[n_y + 1 :]
    q_ref, g_ref, own_w_ref, other_w_ref, keep_ref, send_ref = refs[:6]
    lg_ref, lat, bias, lat_t, total, weight = refs[6:]
    step = pl.program_id(0)
    zh, y, core = place_ref[0], place_ref[1], place_ref[2]
    rows = total.shape[0] // n_y
    tokens = rows // 2

    @pl.when(step == 0)
    def _():
        for k in range(n_y):
            start = pl.multiple_of((k * 2 + zh) * tokens, tokens)
            lat[pl.ds(start, tokens), :] = mine_ref[k * tokens : (k + 1) * tokens]
            start = pl.multiple_of((((y + n_y - k) % n_y) * 2 + 1 - zh) * tokens, tokens)
            lat[pl.ds(start, tokens), :] = lat_refs[k][...]
        key_pos = lax.broadcasted_iota(jnp.int32, (bias.shape[0], 1), 0)
        lane = lax.broadcasted_iota(jnp.int32, (1, bias.shape[1]), 1)
        block = jnp.where(lane >= 128, 2, 0) + zh
        query_pos = block * 128 + (lane & 127)
        bias[...] = jnp.where(key_pos <= query_pos, F32(0.0), F32(-1e30))
        rows_each = RANK // (n_core * n_x * n_zl)
        row = lax.broadcasted_iota(jnp.int32, (RANK, 1), 0)
        col = lax.broadcasted_iota(jnp.int32, (1, RANK), 1)
        inner = row % rows_each
        zl = (row // rows_each) % n_zl
        x = (row // (rows_each * n_zl) + place_ref[4]) % n_x
        away = row // (rows_each * n_zl * n_x)
        owner = core + away * (1 - 2 * core)
        wanted = ((x * n_zl + zl) * n_core + owner) * rows_each + inner
        pick = jnp.where(wanted == col, F32(1.0), F32(0.0)).astype(BF16)
        lat_t[...] = lax.dot_general(pick, lat[:, :RANK], NT, preferred_element_type=F32).astype(
            BF16
        )
        total[...] = jnp.zeros_like(total)

    held = step // (pl.num_programs(0) // 2) == zh

    @pl.when(held)
    def _():
        weight[...] = own_w_ref[...]

    @pl.when(jnp.logical_not(held))
    def _():
        weight[...] = other_w_ref[...]

    w = weight[...]
    kv = jnp.dot(lat[:, :RANK], w, preferred_element_type=F32).astype(BF16)
    weight_parts, latent_sum = head_pair(
        kv, lat[:, RANK : RANK + ROPE], q_ref[...], g_ref[...], w, bias[...], lat_t[...]
    )
    half = RANK // n_core
    for away, ref in enumerate((keep_ref, send_ref)):
        for h in range(2):
            part = weight_parts[h][away * half : (away + 1) * half].reshape(n_x, -1, KVW)
            ref[:, 0, :, h * KVW : (h + 1) * KVW] = part
    total[...] += latent_sum

    @pl.when(step == pl.num_programs(0) - 1)
    def _():
        lg_ref[...] = total[...].astype(BF16)


def attention(place, latents, query_grad, own_weight, other_weight, sizes):
    n_core, n_x, n_zl = sizes
    n_y = len(latents)
    q_rows, width = query_grad.shape[0], latents[0].shape[1]
    length = 2 * q_rows
    heads = 2 * own_weight.shape[1] // KVW
    steps = heads // 2
    g_blocks = heads * QW // (2 * VDIM)
    rows = RANK // (n_core * n_x)
    lat_spec = pl.BlockSpec((q_rows // n_y, width), lambda i, p: (0, 0))
    lat_block = heads * (QW + VDIM) // width
    w_spec = pl.BlockSpec((RANK, 2 * KVW), lambda i, p: (0, i % (steps // 2)))
    grad_spec = pl.BlockSpec(
        (n_x, 1, rows, 2 * KVW), lambda i, p: (0, i // (steps // 2), 0, i % (steps // 2))
    )
    grad_shape = jax.ShapeDtypeStruct((n_x, 2, rows, heads * KVW // 2), BF16)
    latent_spec = pl.BlockSpec((length, RANK), lambda i, p: (0, 0))
    latent_shape = jax.ShapeDtypeStruct((length, RANK), BF16)
    flops = heads * (3 * 2 * length * RANK * KVW + 4 * 2 * length * q_rows * 192)
    return pl.pallas_call(
        functools.partial(attention_kernel, n_core, n_x, n_zl, n_y),
        grid_spec=pltpu.PrefetchScalarGridSpec(
            num_scalar_prefetch=1,
            grid=(steps,),
            in_specs=[
                pl.BlockSpec((q_rows, width), lambda i, p: (0, lat_block)),
                *[lat_spec] * n_y,
                pl.BlockSpec((q_rows, 2 * QW), lambda i, p: (0, i)),
                pl.BlockSpec((q_rows, 2 * VDIM), lambda i, p: (0, g_blocks + i)),
                w_spec,
                w_spec,
            ],
            out_specs=[grad_spec, grad_spec, latent_spec],
            scratch_shapes=[
                pltpu.VMEM((length, width), BF16),
                pltpu.VMEM((length // 2, length // 4), F32),
                pltpu.VMEM((RANK, length), BF16),
                pltpu.VMEM((length, RANK), F32),
                pltpu.VMEM((RANK, 2 * KVW), BF16),
            ],
        ),
        out_shape=[grad_shape, grad_shape, latent_shape],
        compiler_params=pltpu.CompilerParams(
            dimension_semantics=("arbitrary",), vmem_limit_bytes=56 * 2**20
        ),
        cost_estimate=pl.CostEstimate(
            flops=flops, bytes_accessed=16 * 2**20, transcendentals=heads * length * q_rows
        ),
    )(place, query_grad, *latents, query_grad, query_grad, own_weight, other_weight)


def latent_columns(latent_ref, rope_ref):
    rope = rope_ref[...].astype(F32).T.astype(BF16)
    return jnp.concatenate([latent_ref[...], rope, jnp.zeros_like(rope)], axis=1)


def split_kernel(queries_ref, grads_ref, latent_ref, rope_ref, out_ref):
    q_width, g_width = queries_ref.shape[1], grads_ref.shape[1]
    out_ref[0, :, :q_width] = queries_ref[...]
    out_ref[0, :, q_width : q_width + g_width] = grads_ref[...]
    out_ref[0, :, q_width + g_width :] = latent_columns(latent_ref, rope_ref)


def split_heads(queries, out_grad, latent, rope, n_y):
    tokens, rank = latent.shape
    widths = (queries.shape[1] // n_y, out_grad.shape[1] // n_y)
    shape = (n_y, tokens, sum(widths) + rank + 2 * ROPE)
    return pl.pallas_call(
        split_kernel,
        grid=(n_y,),
        in_specs=[
            pl.BlockSpec((tokens, widths[0]), lambda i: (0, i)),
            pl.BlockSpec((tokens, widths[1]), lambda i: (0, i)),
            pl.BlockSpec((tokens, rank), lambda i: (0, 0)),
            pl.BlockSpec((ROPE, tokens), lambda i: (0, 0)),
        ],
        out_specs=pl.BlockSpec((1,) + shape[1:], lambda i: (i, 0, 0)),
        out_shape=jax.ShapeDtypeStruct(shape, BF16),
        cost_estimate=pl.CostEstimate(
            flops=0, bytes_accessed=4 * math.prod(shape), transcendentals=0
        ),
    )(queries, out_grad, latent, rope.T)


def pack_kernel(place_ref, latent_ref, rope_ref, weight_ref, out_ref):
    tokens, rank = latent_ref.shape
    out_ref[:, : rank + 2 * ROPE] = latent_columns(latent_ref, rope_ref)
    rows, width = weight_ref.shape
    width = width * rows // tokens
    for k in range(tokens // rows):
        columns = weight_ref[:, k * width : (k + 1) * width]
        out_ref[k * rows : (k + 1) * rows, rank + 2 * ROPE :] = columns


def pack(place, latent, rope, weight, pieces):
    tokens, rank = latent.shape
    rows, width = weight.shape[0] // pieces, weight.shape[1]
    shape = (tokens, rank + 2 * ROPE + width * rows // tokens)
    return pl.pallas_call(
        pack_kernel,
        grid_spec=pltpu.PrefetchScalarGridSpec(
            num_scalar_prefetch=1,
            grid=(1,),
            in_specs=[
                pl.BlockSpec((tokens, rank), lambda i, p: (0, 0)),
                pl.BlockSpec((ROPE, tokens), lambda i, p: (0, 0)),
                pl.BlockSpec((rows, width), lambda i, p: (p[3], 0)),
            ],
            out_specs=pl.BlockSpec(shape, lambda i, p: (0, 0)),
        ),
        out_shape=jax.ShapeDtypeStruct(shape, BF16),
        cost_estimate=pl.CostEstimate(
            flops=0, bytes_accessed=4 * math.prod(shape), transcendentals=0
        ),
    )(place, latent, rope.T, weight)


def unpack_kernel(other_ref, lat_ref, weight_ref):
    width = lat_ref.shape[1]
    lat_ref[...] = other_ref[:, :width]
    count, rows, columns = weight_ref.shape
    blocks = lat_ref.shape[0] // rows
    columns = columns // blocks
    for k in range(count):
        for block in range(blocks):
            part = other_ref[block * rows : (block + 1) * rows, width:]
            weight_ref[k, :, block * columns : (block + 1) * columns] = part


def unpack(other, count, piece_rows):
    tokens, width = other.shape
    latent_width = RANK + 2 * ROPE
    piece = (count, piece_rows, (width - latent_width) * tokens // piece_rows)
    return pl.pallas_call(
        unpack_kernel,
        out_shape=[
            jax.ShapeDtypeStruct((tokens, latent_width), BF16),
            jax.ShapeDtypeStruct(piece, BF16),
        ],
        cost_estimate=pl.CostEstimate(
            flops=0, bytes_accessed=3 * math.prod(piece), transcendentals=0
        ),
    )(other)


def rotate(array, axis, shift):
    n = lax.axis_size(axis)
    return lax.ppermute(array, axis, [(i, (i + shift) % n) for i in range(n)])


def exchange(pieces, axes):
    return lax.all_to_all(pieces, axes, split_axis=0, concat_axis=0, tiled=True)


def add_up(pieces, dtype=BF16):
    return jnp.sum(pieces.astype(F32), axis=0).astype(dtype)


def per_device(queries, latent, key_rope, up_weight, out_grad):
    n_x, n_zl, n_core = lax.axis_size("x"), lax.axis_size(ZL), lax.axis_size("core")
    n_y, n_zh = lax.axis_size("y"), lax.axis_size("zh")
    zh, y, core = lax.axis_index("zh"), lax.axis_index("y"), lax.axis_index("core")
    mine = lax.axis_index(HOLDERS)
    place = jnp.stack([zh, y, core, mine, lax.axis_index("x")]).astype(jnp.int32)
    tokens = latent.shape[0]
    pieces = lax.axis_size(HOLDERS)

    packed = pack(place, latent, key_rope, up_weight, pieces)
    sent = split_heads(queries, out_grad, latent, key_rope, n_y)
    query_grad = exchange(sent, "y").reshape(n_y * tokens, -1)
    latents, piece = unpack(rotate(packed, "zh", 1), pieces, RANK // pieces)
    latents = [latents] + [rotate(latents, "y", k + 1) for k in range(n_y - 1)]
    piece, query_grad = lax.optimization_barrier((piece, query_grad))
    other_weight = exchange(piece, HOLDERS).reshape(up_weight.shape)

    sizes = (n_core, n_x, n_zl)
    keep, send, latent_part = attention(place, latents, query_grad, up_weight, other_weight, sizes)
    away = rotate(send, "core", 1)
    on_chip = [(keep[k].astype(F32) + away[k].astype(F32)).astype(BF16) for k in range(n_x)]

    arrived = exchange(latent_part.reshape(n_y, n_zh * tokens, RANK), "y")
    latent_sum = add_up(arrived, F32).reshape(n_zh, tokens, RANK)
    sent = lax.dynamic_index_in_dim(latent_sum, 1 - zh, 0, keepdims=False).astype(BF16)
    kept = lax.dynamic_index_in_dim(latent_sum, zh, 0, keepdims=False)
    sent = rotate(sent, "zh", 1)
    over_x = [on_chip[0]] + [rotate(a, "x", k + 1) for k, a in enumerate(on_chip[1:])]
    over_x = sum(a.astype(F32) for a in over_x).astype(BF16)
    rows = over_x.shape[1] // n_zl
    pieces = over_x.reshape(n_zh, n_zl, rows, -1).swapaxes(0, 1)
    over_zl = add_up(exchange(pieces, ZL), F32)
    latent_grad = kept + sent.astype(F32)
    own = lax.dynamic_index_in_dim(over_zl, zh, 0, keepdims=False)
    other = lax.dynamic_index_in_dim(over_zl, 1 - zh, 0, keepdims=False)
    weight_grad = own + rotate(other, "zh", 1)
    return latent_grad, weight_grad * (1.0 / (n_x * n_zl * n_core))


def solution(mesh):
    replicas, parts = mesh.shape["dp"], mesh.shape["seq"]
    shape = (replicas // 16, 4, 2, 2, parts // 2, 2)
    names = ("x", *ZL, "core", "y", "zh")
    torus = Mesh(mesh.devices.reshape(shape), names)
    rows = P(names, None)
    in_specs = (rows, rows, rows, P(None, ("y", "zh")), rows)
    out_specs = (rows, P(("x", *ZL, "core"), ("y", "zh")))
    return jax.shard_map(
        per_device, mesh=torus, in_specs=in_specs, out_specs=out_specs, check_vma=False
    )
```
